32 devices in a mesh: row: 8 (over z, x), col: 4 (over y, core).
Axes of the slice: x: 2, y: 2, z: 4, core: 2. Of those that a mesh axis runs over, the one named last changes fastest.
Arguments:
- features: bfloat16 [2048, 512], P(('row', 'col')), may hold values from -0.5 to 0.5
- slot_of_ray: int32 [2048], P(('row', 'col')), may hold values from 0 to 63
- noise: float32 [2048], P(('row', 'col')), may hold values from 0.2 to 1
Outputs:
- front: float32 [2048, 4, 512], P('row', 'col')
- factor: float32 [2048, 1024], P('row')
The draws below stay inside these ranges and needn't reach their ends.
All inputs are finite; a program needn't handle non-finite values.
Results may differ from the reference program's by a relative error of at most 0.0003.
Values may be sent and summed in bfloat16 or wider, within the bound.
No kernel may reach another device: no remote copies, remote signals or barrier semaphores. Data moves between devices by JAX's collectives and lax.ppermute only.
A program may use at most 64 MiB of HBM per device.

```python
import math
import jax
import jax.numpy as jnp
from jax import lax

RAY_DEV = 64
F = 512
PANEL = 256
PANELS = 4
NT = 64
RAYS = 2048
N_ROW = 8
N_COL = 4


def touch_ends(entries, own_key, low, largest):
    longest = entries.shape.index(max(entries.shape))
    spots = []
    for shift in (0, 1):
        where = [jax.random.randint(jax.random.fold_in(own_key, axis), (), 0, length) for axis, length in enumerate(entries.shape)]
        where[longest] = (where[longest] + shift) % entries.shape[longest]
        spots.append(tuple(where))
    return entries.at[spots[0]].set(low).at[spots[1]].set(largest)


def block_levels(rng, dims, shards, smallest, high):
    def one(axis_at, parts):
        steps = jax.random.uniform(jax.random.fold_in(jax.random.fold_in(rng, 6), axis_at), (parts,), jnp.float32, smallest / len(shards), high / len(shards))
        return jnp.repeat(jnp.exp(steps), dims[axis_at] // parts).reshape((-1,) + (1,) * (len(dims) - axis_at - 1))

    factor_of = one(*shards[0])
    for cut in shards[1:]:
        factor_of = factor_of * one(*cut)
    return factor_of


def normal_values(rng, shape, scale, limit, cuts=(), kind=jnp.bfloat16):
    factor_of = block_levels(rng, shape, cuts, -0.22, 0.18) if cuts else 1.0
    values = jax.random.normal(rng, shape, jnp.float32) * scale * factor_of
    return jnp.minimum(jnp.maximum(values, -limit), limit).astype(kind)


def setup_inputs(seed: int = 0) -> dict:
    key_list = jax.random.split(jax.random.key(seed), 4)
    return {
        "features": normal_values(key_list[0], (RAYS, F), (F // 4) ** -0.5, 0.5, ((0, 32),)),
        "slot_of_ray": touch_ends(jax.random.randint(key_list[1], (RAYS,), 0, NT), jax.random.fold_in(key_list[1], 1), 0, NT - 1).astype(jnp.int32),
        "noise": jnp.clip(jnp.exp(math.log(1.0) - 1.609438 * jax.random.uniform(key_list[2], (RAYS,), jnp.float32) ** block_levels(key_list[2], (RAYS,), ((0, 32),), -0.2, 0.2)), 0.2, 1.0),
    }


def time_rate():
    length = NT / 8.0
    return 1.0 / (2.0 * length * length)

def reference(features, slot_of_ray, noise):
    slot_values = slot_of_ray.astype(jnp.float32)
    gram_tile = lax.dot_general(features.astype(jnp.float32), features.astype(jnp.float32), (((1,), (1,)), ((), ())), preferred_element_type=jnp.float32)
    slot_gap = slot_values[:, None] - slot_values[None, :]
    complement = gram_tile * jnp.exp(-slot_gap * slot_gap * time_rate())
    ray_rows = jnp.arange(RAYS, dtype=jnp.int32)
    complement = complement.at[ray_rows, ray_rows].add(noise)
    columns = []
    for panel_number in range(PANELS):
        panel_start = panel_number * PANEL
        panel_top = complement[panel_start:panel_start + PANEL]
        triangle = jnp.linalg.cholesky(panel_top[:, panel_start:panel_start + PANEL])
        solved = jax.scipy.linalg.solve_triangular(triangle, panel_top, lower=True)
        complement = complement - lax.dot_general(solved.astype(jnp.float32), solved.astype(jnp.float32), (((0,), (0,)), ((), ())), precision=lax.Precision.HIGHEST, preferred_element_type=jnp.float32)
        below_mask = ray_rows[:, None] >= panel_start + jnp.arange(PANEL, dtype=jnp.int32)[None, :]
        columns.append(jnp.where(below_mask, solved.T, 0.0))
    factor = jnp.concatenate(columns, axis=1)
    eliminated = PANELS * PANEL
    remaining = (ray_rows[:, None] >= eliminated) & (ray_rows[None, :] >= eliminated)
    front_out = jnp.where(remaining, complement, 0.0)
    front_out = front_out.reshape(RAYS, N_ROW, N_COL, RAY_DEV).transpose(0, 2, 1, 3).reshape(RAYS, N_COL, N_ROW * RAY_DEV)
    return (front_out, factor)
```

```python
import functools

import jax
import jax.numpy as jnp
from jax import lax
from jax.experimental import pallas as pl
from jax.experimental.pallas import tpu as pltpu
from jax.sharding import PartitionSpec as P

PANEL = 256
PANELS = 4
NT = 64
LANES = 128
SUBS = 8
HALF = PANEL // 2
HIGH = lax.Precision.HIGHEST


def time_rate():
    length = NT / 8.0
    return 1.0 / (2.0 * length * length)


def dot(a, b, ca, cb, precision=HIGH):
    return lax.dot_general(
        a, b, (((ca,), (cb,)), ((), ())), precision=precision, preferred_element_type=jnp.float32
    )


def inverse_factor(block):
    count = block.shape[0] // SUBS
    strips = [block[SUBS * t : SUBS * (t + 1), :] for t in range(count)]
    shape = (SUBS, LANES)
    lane = lax.broadcasted_iota(jnp.int32, shape, 1)
    sub = lax.broadcasted_iota(jnp.int32, shape, 0)

    def over_subs(x, k):
        return jnp.broadcast_to(x[k : k + 1, :], shape)

    def over_lanes(x, j):
        return jnp.broadcast_to(x[:, j : j + 1], shape)

    result = []
    for s in range(count):
        base = SUBS * s
        corner = [over_lanes(strips[s], base + j) for j in range(SUBS)]
        own = (lane >= base) & (lane < base + SUBS)
        rows = jnp.where(own, jnp.where(lane - base == sub, 1.0, 0.0), strips[s])
        scaled = rows
        pivots = rows
        for k in range(SUBS):
            pivot = over_subs(corner[k], k)
            inverse = 1.0 / pivot
            lead_row = over_subs(rows, k) * inverse
            here = sub == k
            scaled = jnp.where(here, lead_row, scaled)
            pivots = jnp.where(here, pivot, pivots)
            rows = jnp.where(here, lead_row, rows - corner[k] * lead_row)
            for j in range(k + 1, SUBS):
                entry = over_subs(corner[k], j) * inverse
                corner[j] = jnp.where(here, entry, corner[j] - corner[k] * entry)
        result.append(jnp.where(lane - base <= sub, scaled * jnp.sqrt(pivots), 0.0))
        lead_rows = [over_subs(rows, k) for k in range(SUBS)]
        for t in range(s + 1, count):
            terms = [over_lanes(strips[t], base + k) * lead_rows[k] for k in range(SUBS)]
            while len(terms) > 1:
                terms = [a + b for a, b in zip(terms[::2], terms[1::2])]
            strips[t] = jnp.where(own, 0.0, strips[t]) - terms[0]
    return jnp.concatenate(result, axis=0)


def covariance(feat_a, feat_b, slot_a, slot_b, ray_a, ray_b, noise_b):
    gram = dot(feat_a, feat_b, 1, 1, None)
    gap = slot_a - slot_b
    tile = gram * jnp.exp(-gap * gap * time_rate())
    return tile + jnp.where(ray_a == ray_b, noise_b, 0.0)


def as_column(row):
    return jnp.broadcast_to(row, (LANES, row.shape[1])).T


def kernel(
    lead_feat, row_feat, col_feat, lead_aux, row_aux, col_aux, front, factor, mat, upper, inv
):
    lead = lead_feat.shape[0]
    rows, cols = row_feat.shape[0], col_feat.shape[0]
    row_tiles, col_tiles = rows // PANEL, cols // LANES
    skipped = front.shape[1] - cols

    def fill(feat_ref, aux_ref, count, start):
        @pl.loop(0, count)
        def _(i):
            at = pl.multiple_of(i * LANES, LANES)
            a = feat_ref[pl.ds(at, LANES), :]
            slot_a = as_column(aux_ref[0:1, pl.ds(at, LANES)])
            ray_a = as_column(aux_ref[2:3, pl.ds(at, LANES)])
            to = pl.multiple_of(start + at, LANES)

            @pl.loop(0, lead // LANES)
            def _(j):
                b = pl.multiple_of(j * LANES, LANES)
                mat[pl.ds(to, LANES), pl.ds(b, LANES)] = covariance(
                    a,
                    lead_feat[pl.ds(b, LANES), :],
                    slot_a,
                    lead_aux[0:1, pl.ds(b, LANES)],
                    ray_a,
                    lead_aux[2:3, pl.ds(b, LANES)],
                    lead_aux[1:2, pl.ds(b, LANES)],
                )

            @pl.loop(0, col_tiles)
            def _(j):
                b = pl.multiple_of(j * LANES, LANES)
                mat[pl.ds(to, LANES), pl.ds(pl.multiple_of(lead + b, LANES), LANES)] = covariance(
                    a,
                    col_feat[pl.ds(b, LANES), :],
                    slot_a,
                    col_aux[0:1, pl.ds(b, LANES)],
                    ray_a,
                    col_aux[2:3, pl.ds(b, LANES)],
                    col_aux[1:2, pl.ds(b, LANES)],
                )

    fill(lead_feat, lead_aux, lead // LANES, 0)
    fill(row_feat, row_aux, rows // LANES, lead)

    panels = lead // PANEL
    width = lead + cols

    @pl.loop(0, panels)
    def _(p):
        at = pl.multiple_of(p * PANEL, PANEL)
        mid = pl.multiple_of(at + HALF, HALF)
        inv_a = inverse_factor(mat[pl.ds(at, HALF), pl.ds(at, HALF)])
        cross = dot(inv_a, mat[pl.ds(at, HALF), pl.ds(mid, HALF)], 1, 0)
        inv_b = inverse_factor(
            mat[pl.ds(mid, HALF), pl.ds(mid, HALF)] - dot(cross, cross, 0, 0)
        )
        inv[0:HALF, 0:HALF] = inv_a
        inv[0:HALF, HALF:PANEL] = jnp.zeros((HALF, HALF), jnp.float32)
        inv[HALF:PANEL, HALF:PANEL] = inv_b
        inv[HALF:PANEL, 0:HALF] = -dot(inv_b, dot(cross, inv_a, 0, 0), 1, 0)

        first = (at + PANEL) // LANES

        @pl.loop(first, width // LANES)
        def _(j):
            b = pl.multiple_of(j * LANES, LANES)
            upper[:, pl.ds(b, LANES)] = dot(
                inv[...], mat[pl.ds(at, PANEL), pl.ds(b, LANES)], 1, 0
            )

        @pl.loop(p + 1, panels)
        def _(q):
            row = pl.multiple_of(q * PANEL, PANEL)
            lower = upper[:, pl.ds(row, PANEL)]

            @pl.loop(row // LANES, width // LANES)
            def _(j):
                b = pl.multiple_of(j * LANES, LANES)
                mat[pl.ds(row, PANEL), pl.ds(b, LANES)] -= dot(
                    lower, upper[:, pl.ds(b, LANES)], 0, 0
                )

        @pl.loop(0, row_tiles)
        def _(i):
            here = pl.multiple_of(i * PANEL, PANEL)
            row = pl.multiple_of(lead + here, PANEL)
            solved = dot(mat[pl.ds(row, PANEL), pl.ds(at, PANEL)], inv[...], 1, 1)
            ray = as_column(row_aux[2:3, pl.ds(here, PANEL)])
            for half in range(2):
                offset = at + half * LANES
                lanes = lax.broadcasted_iota(jnp.int32, (PANEL, LANES), 1) + offset
                factor[pl.ds(here, PANEL), pl.ds(pl.multiple_of(offset, LANES), LANES)] = jnp.where(
                    ray >= lanes.astype(jnp.float32),
                    solved[:, half * LANES : (half + 1) * LANES],
                    0.0,
                )

            @pl.loop(first, width // LANES)
            def _(j):
                b = pl.multiple_of(j * LANES, LANES)
                mat[pl.ds(row, PANEL), pl.ds(b, LANES)] -= dot(
                    solved, upper[:, pl.ds(b, LANES)], 1, 0
                )

    if skipped:
        front[:, 0:skipped] = jnp.zeros((rows, skipped), jnp.float32)
    keep = row_aux[2, 0] >= lead

    @pl.loop(0, col_tiles)
    def _(j):
        b = pl.multiple_of(j * LANES, LANES)
        front[:, pl.ds(pl.multiple_of(skipped + b, LANES), LANES)] = jnp.where(
            keep, mat[pl.ds(lead, rows), pl.ds(pl.multiple_of(lead + b, LANES), LANES)], 0.0
        )


def shards(features, slot_of_ray, noise):
    ray_dev = noise.shape[0]
    row_count, col_count = lax.axis_size("row"), lax.axis_size("col")
    row_width, col_width = ray_dev * col_count, ray_dev * row_count
    row_index, col_index = lax.axis_index("row"), lax.axis_index("col")
    lead = PANELS * PANEL
    own = jnp.concatenate([slot_of_ray.astype(jnp.float32), noise])[None]
    every = lax.all_gather(features, ("row", "col"), axis=0, tiled=True)
    aux = lax.all_gather(own, ("row", "col"), axis=0, tiled=True)
    rays = row_count * row_width
    aux = aux.reshape(rays // ray_dev, 2, ray_dev).transpose(1, 0, 2).reshape(2, rays)
    aux = jnp.concatenate([aux, jnp.arange(rays, dtype=jnp.float32)[None]])
    skipped_blocks = lead // row_width
    row_feat = lax.dynamic_slice_in_dim(every, row_index * row_width, row_width, 0)
    row_aux = lax.dynamic_slice_in_dim(aux, row_index * row_width, row_width, 1)
    blocks = every.reshape(row_count, col_count, ray_dev, -1)[skipped_blocks:]
    col_feat = lax.dynamic_index_in_dim(blocks, col_index, 1, False).reshape(-1, features.shape[1])
    aux_blocks = aux.reshape(3, row_count, col_count, ray_dev)[:, skipped_blocks:]
    col_aux = lax.dynamic_index_in_dim(aux_blocks, col_index, 2, False).reshape(3, -1)
    cols = col_feat.shape[0]
    front, factor = pl.pallas_call(
        kernel,
        out_shape=(
            jax.ShapeDtypeStruct((row_width, col_width), jnp.float32),
            jax.ShapeDtypeStruct((row_width, lead), jnp.float32),
        ),
        scratch_shapes=[
            pltpu.VMEM((lead + row_width, lead + cols), jnp.float32),
            pltpu.VMEM((PANEL, lead + cols), jnp.float32),
            pltpu.VMEM((PANEL, PANEL), jnp.float32),
        ],
        name="panels",
    )(every[:lead], row_feat, col_feat, aux[:, :lead], row_aux, col_aux)
    return front.reshape(row_width, 1, col_width), factor


def solution(mesh):
    return jax.shard_map(
        shards,
        mesh=mesh,
        in_specs=(P(("row", "col"), None), P(("row", "col")), P(("row", "col"))),
        out_specs=(P("row", "col", None), P("row", None)),
        check_vma=False,
    )
```

```python
import functools

import jax
import jax.numpy as jnp
from jax import lax
from jax.experimental import pallas as pl
from jax.experimental.pallas import tpu as pltpu
from jax.sharding import PartitionSpec as P

PANEL = 256
PANELS = 4
NT = 64
LANES = 128
SUBS = 8
HALF = PANEL // 2


def time_rate():
    length = NT / 8.0
    return 1.0 / (2.0 * length * length)


def dot(a, b, ca, cb):
    return lax.dot_general(
        a,
        b,
        (((ca,), (cb,)), ((), ())),
        precision=lax.Precision.HIGHEST,
        preferred_element_type=jnp.float32,
    )


def inverse_factor(block):
    count = block.shape[0] // SUBS
    strips = [block[SUBS * t : SUBS * (t + 1), :] for t in range(count)]
    shape = (SUBS, LANES)
    lane = lax.broadcasted_iota(jnp.int32, shape, 1)
    sub = lax.broadcasted_iota(jnp.int32, shape, 0)

    def over_subs(x, k):
        return jnp.broadcast_to(x[k : k + 1, :], shape)

    def over_lanes(x, j):
        return jnp.broadcast_to(x[:, j : j + 1], shape)

    result = []
    for s in range(count):
        base = SUBS * s
        corner = [over_lanes(strips[s], base + j) for j in range(SUBS)]
        own = (lane >= base) & (lane < base + SUBS)
        rows = jnp.where(own, jnp.where(lane - base == sub, 1.0, 0.0), strips[s])
        scaled = rows
        pivots = rows
        for k in range(SUBS):
            pivot = over_subs(corner[k], k)
            inverse = 1.0 / pivot
            lead_row = over_subs(rows, k) * inverse
            here = sub == k
            scaled = jnp.where(here, lead_row, scaled)
            pivots = jnp.where(here, pivot, pivots)
            rows = jnp.where(here, lead_row, rows - corner[k] * lead_row)
            for j in range(k + 1, SUBS):
                entry = over_subs(corner[k], j) * inverse
                corner[j] = jnp.where(here, entry, corner[j] - corner[k] * entry)
        result.append(jnp.where(lane - base <= sub, scaled * jnp.sqrt(pivots), 0.0))
        lead_rows = [over_subs(rows, k) for k in range(SUBS)]
        for t in range(s + 1, count):
            terms = [over_lanes(strips[t], base + k) * lead_rows[k] for k in range(SUBS)]
            while len(terms) > 1:
                terms = [a + b for a, b in zip(terms[::2], terms[1::2])]
            strips[t] = jnp.where(own, 0.0, strips[t]) - terms[0]
    return jnp.concatenate(result, axis=0)


def as_column(row):
    return jnp.broadcast_to(row, (LANES, LANES)).T


def reversed_bits(value, bits):
    out = 0
    for k in range(bits):
        out = out | (((value >> k) & 1) << (bits - 1 - k))
    return out


def bits_of(count):
    return count.bit_length() - 1


def kernel(*refs, ray_dev, row_count, col_count, lead, tops):
    near, near_x = refs[:2]
    lists = [refs[2 + k * tops : 2 + (k + 1) * tops] for k in range(4)]
    side, side_x, core, core_x = lists
    front, factor, feat, slot, noise, ray, mat, upper, inv = refs[2 + 4 * tops :]
    row_index, col_index = lax.axis_index("row"), lax.axis_index("col")
    rows = ray_dev * col_count
    pair_count = near.shape[0]
    lead_pairs = lead // rows // 2
    cols = (pair_count - lead_pairs) * 2 * ray_dev
    row_pair, odd_row = row_index // 2, row_index % 2
    col_pair, odd_col = col_index // 2, col_index % 2
    lanes = lax.broadcasted_iota(jnp.int32, (1, LANES), 1)

    def aux_of(block):
        line = block[ray_dev : ray_dev + SUBS, :].astype(jnp.float32)[0:1]
        parts = [line[:, LANES * k : LANES * (k + 1)] for k in range(4)]
        return parts[0], parts[1] + parts[2] + parts[3]

    def put(mine, other, odd, to, numbers):
        here = pl.multiple_of(to + odd * ray_dev, ray_dev)
        there = pl.multiple_of(to + (1 - odd) * ray_dev, ray_dev)
        feat[pl.ds(here, ray_dev), :] = mine[:ray_dev, :]
        feat[pl.ds(there, ray_dev), :] = other[:ray_dev, :]
        tile = to // LANES
        for out, a, b in zip((slot, noise), aux_of(mine), aux_of(other)):
            even, late = jnp.where(odd == 0, a, b), jnp.where(odd == 0, b, a)
            out[pl.ds(tile, 1), :] = even + pltpu.roll(late, ray_dev, 1)
        ray[pl.ds(tile, 1), :] = numbers.astype(jnp.float32)

    low_bits = bits_of(lead_pairs)
    for k in range(lead_pairs):
        pair = (row_pair % lead_pairs) ^ reversed_bits(k, low_bits)
        for bit in range(2):
            row = pair * 2 + (odd_row if bit == 0 else 1 - odd_row)
            for top in range(tops):
                at = (col_pair ^ reversed_bits(top, bits_of(tops))) * LANES + row * rows
                mine, other = (side, core) if bit == 0 else (side_x, core_x)
                put(mine[top][k], other[top][k], odd_col, at, lanes + at)
    for top in range(tops):
        at = (col_pair ^ reversed_bits(top, bits_of(tops))) * LANES
        numbers = lanes + (row_index * rows + at)
        put(side[top][lead_pairs], core[top][lead_pairs], odd_col, lead + at, numbers)
    for place in range(pair_count):
        pair = row_pair ^ reversed_bits(place, bits_of(pair_count))

        @pl.when(pair >= lead_pairs)
        def _():
            numbers = ((pair * 2 + lanes // ray_dev) * col_count + col_index) * ray_dev
            numbers = numbers + lanes % ray_dev
            at = lead + rows + (pair - lead_pairs) * LANES
            put(near[place], near_x[place], odd_row, at, numbers)

    if cols % PANEL:
        feat[lead + rows + cols :, :] = jnp.zeros((PANEL - cols % PANEL, feat.shape[1]), feat.dtype)
        for out in (slot, noise, ray):
            out[(lead + rows + cols) // LANES :, :] = jnp.full((1, LANES), -1.0, jnp.float32)

    panels, row_tiles = lead // PANEL, rows // PANEL
    col_tiles = (cols + PANEL - 1) // PANEL
    wide = panels + col_tiles

    def tile(i):
        return pl.ds(pl.multiple_of(i * PANEL, PANEL), PANEL)

    def column(source, i):
        return jnp.concatenate([as_column(source[pl.ds(2 * i + k, 1), :]) for k in range(2)], axis=0)

    def line(source, i):
        return [source[pl.ds(2 * i + k, 1), :] for k in range(2)]

    def spot(j):
        return jnp.where(j < panels, j, j + row_tiles)

    def tile_of(i, j, slot_a, ray_a):
        gram = lax.dot_general(
            feat[tile(i), :],
            feat[tile(j), :],
            (((1,), (1,)), ((), ())),
            preferred_element_type=jnp.float32,
        )
        halves = []
        slots, noises, rays = line(slot, j), line(noise, j), line(ray, j)
        for k in range(2):
            gap = slot_a - slots[k]
            part = gram[:, k * LANES : (k + 1) * LANES] * jnp.exp(-gap * gap * time_rate())
            halves.append(part + jnp.where(ray_a == rays[k], noises[k], 0.0))
        return jnp.concatenate(halves, axis=1)

    @pl.loop(0, panels + row_tiles)
    def _(i):
        slot_a, ray_a = column(slot, i), column(ray, i)

        @pl.loop(jnp.where(i < panels, i, 0), wide)
        def _(j):
            mat[tile(i), tile(j)] = tile_of(i, spot(j), slot_a, ray_a)

    @pl.loop(0, panels)
    def _(p):
        at = pl.multiple_of(p * PANEL, PANEL)
        mid = pl.multiple_of(at + HALF, HALF)
        inv_a = inverse_factor(mat[pl.ds(at, HALF), pl.ds(at, HALF)])
        cross = dot(inv_a, mat[pl.ds(at, HALF), pl.ds(mid, HALF)], 1, 0)
        inv_b = inverse_factor(mat[pl.ds(mid, HALF), pl.ds(mid, HALF)] - dot(cross, cross, 0, 0))
        inv[0:HALF, 0:HALF] = inv_a
        inv[0:HALF, HALF:PANEL] = jnp.zeros((HALF, HALF), jnp.float32)
        inv[HALF:PANEL, HALF:PANEL] = inv_b
        inv[HALF:PANEL, 0:HALF] = -dot(inv_b, dot(cross, inv_a, 0, 0), 1, 0)

        @pl.loop(p + 1, wide)
        def _(j):
            upper[:, tile(j)] = dot(inv[...], mat[tile(p), tile(j)], 1, 0)

        @pl.loop(p + 1, panels)
        def _(q):
            @pl.loop(q, wide)
            def _(j):
                mat[tile(q), tile(j)] -= dot(upper[:, tile(q)], upper[:, tile(j)], 0, 0)

        @pl.loop(0, row_tiles)
        def _(i):
            solved = dot(mat[tile(panels + i), tile(p)], inv[...], 1, 1)
            ray_a = column(ray, panels + i)
            kept = [
                jnp.where(ray_a >= line_k, solved[:, k * LANES : (k + 1) * LANES], 0.0)
                for k, line_k in enumerate(line(ray, p))
            ]
            factor[tile(i), tile(p)] = jnp.concatenate(kept, axis=1)

            @pl.loop(p + 1, wide)
            def _(j):
                mat[tile(panels + i), tile(j)] -= dot(solved, upper[:, tile(j)], 1, 0)

    skipped = front.shape[1] - cols
    front[:, 0:skipped] = jnp.zeros((rows, skipped), jnp.float32)
    front[:, skipped:] = jnp.where(
        row_index * rows >= lead, mat[lead : lead + rows, lead : lead + cols], 0.0
    )


def packed(features, slot_of_ray, noise):
    high = lax.reduce_precision(noise, 8, 7)
    middle = lax.reduce_precision(noise - high, 8, 7)
    terms = jnp.stack([slot_of_ray.astype(jnp.float32), high, middle, noise - high - middle])
    ray_dev, width = features.shape
    aux = jnp.pad(terms, ((0, 0), (0, LANES - ray_dev))).reshape(1, 4 * LANES)
    aux = jnp.pad(aux, ((0, SUBS - 1), (0, width - 4 * LANES))).astype(features.dtype)
    return jnp.concatenate([features, aux])


def shards(features, slot_of_ray, noise):
    ray_dev = noise.shape[0]
    row_count, col_count = lax.axis_size("row"), lax.axis_size("col")
    rows, col_width = ray_dev * col_count, ray_dev * row_count
    row_index = lax.axis_index("row")
    lead = PANELS * PANEL
    row_bits, col_bits = bits_of(row_count), bits_of(col_count)
    tops = col_count // 2
    lead_pairs = lead // rows // 2

    def other(value, axis, bit):
        count = lax.axis_size(axis)
        return lax.ppermute(value, axis, [(k, k ^ (1 << bit)) for k in range(count)])

    near = packed(features, slot_of_ray, noise)[None]
    own = near
    for bit in reversed(range(1, row_bits)):
        near = jnp.concatenate([near, other(near, "row", bit)])
    high_bits = row_bits - 1 - bits_of(lead_pairs)
    group = reversed_bits(row_index >> (row_bits - high_bits), high_bits)

    def leading(blocks):
        split = blocks.reshape(lead_pairs, 1 << high_bits, *blocks.shape[1:])
        return lax.dynamic_index_in_dim(split, group, 1, False)

    near_x = other(near, "row", 0)
    side = [jnp.concatenate([leading(near), own])]
    side_x = [leading(near_x)]
    for bit in reversed(range(1, col_bits)):
        side += [other(value, "col", bit) for value in side]
        side_x += [other(value, "col", bit) for value in side_x]
    core = [other(value, "col", 0) for value in side]
    core_x = [other(value, "col", 0) for value in side_x]

    cols = col_width - lead // col_count
    padded = -(-cols // PANEL) * PANEL
    rays = lead + rows + padded
    front, factor = pl.pallas_call(
        functools.partial(
            kernel, ray_dev=ray_dev, row_count=row_count, col_count=col_count, lead=lead, tops=tops
        ),
        out_shape=(
            jax.ShapeDtypeStruct((rows, col_width), jnp.float32),
            jax.ShapeDtypeStruct((rows, lead), jnp.float32),
        ),
        scratch_shapes=[
            pltpu.VMEM((rays, features.shape[1]), features.dtype),
            *[pltpu.VMEM((rays // LANES, LANES), jnp.float32)] * 3,
            pltpu.VMEM((lead + rows, lead + padded), jnp.float32),
            pltpu.VMEM((PANEL, lead + padded), jnp.float32),
            pltpu.VMEM((PANEL, PANEL), jnp.float32),
        ],
        name="panels",
    )(near, near_x, *side, *side_x, *core, *core_x)
    return front.reshape(rows, 1, col_width), factor


def solution(mesh):
    return jax.shard_map(
        shards,
        mesh=mesh,
        in_specs=(P(("row", "col"), None), P(("row", "col")), P(("row", "col"))),
        out_specs=(P("row", "col", None), P("row", None)),
        check_vma=False,
    )
```

```python
import functools

import jax
import jax.numpy as jnp
from jax import lax
from jax.experimental import pallas as pl
from jax.experimental.pallas import tpu as pltpu
from jax.sharding import PartitionSpec as P

PANEL = 256
PANELS = 4
NT = 64
LANES = 128
SUBS = 8
HALF = PANEL // 2


def time_rate():
    length = NT / 8.0
    return 1.0 / (2.0 * length * length)


def terms_of(value):
    high = value.astype(jnp.bfloat16)
    rest = value - high.astype(jnp.float32)
    middle = rest.astype(jnp.bfloat16)
    low = (rest - middle.astype(jnp.float32)).astype(jnp.bfloat16)
    return high, middle, low


def left(value):
    high, middle, low = terms_of(value)
    return jnp.concatenate([low, high, middle, middle, high, high], axis=1)


def right(value):
    high, middle, low = terms_of(value)
    return jnp.concatenate([high, low, middle, high, middle, high], axis=0)


def product(a, b):
    return jnp.dot(a, b, preferred_element_type=jnp.float32)


def inverse_factor(block):
    count = block.shape[0] // SUBS
    strips = [block[SUBS * t : SUBS * (t + 1), :] for t in range(count)]
    shape = (SUBS, LANES)
    lane = lax.broadcasted_iota(jnp.int32, shape, 1)
    sub = lax.broadcasted_iota(jnp.int32, shape, 0)

    def over_subs(x, k):
        return jnp.broadcast_to(x[k : k + 1, :], shape)

    def over_lanes(x, j):
        return jnp.broadcast_to(x[:, j : j + 1], shape)

    per = count // 2
    result = []
    for s in range(count):
        base = SUBS * s
        raw = [over_lanes(strips[s], base + j) for j in range(SUBS)]
        corner = list(raw)
        own = (lane >= base) & (lane < base + SUBS)
        rows = jnp.where(own, jnp.where(lane - base == sub, 1.0, 0.0), strips[s])
        scaled = rows
        pivots = rows
        for k in range(0, SUBS, 2):
            here, after = sub == k, sub == k + 1
            a, b, c = over_subs(raw[k], k), over_subs(raw[k], k + 1), over_subs(raw[k + 1], k + 1)
            det = a * c - b * b
            inv_a, inv_det = 1.0 / a, 1.0 / det
            ratio = b * inv_a
            plain = corner[k + 1] - corner[k] * ratio
            second = jnp.where(here, ratio, plain)
            row = over_subs(rows, k) * inv_a
            rows = jnp.where(here, row, rows - corner[k] * row)
            row_2 = over_subs(rows, k + 1) * (a * inv_det)
            rows = jnp.where(after, row_2, rows - second * row_2)
            scaled = jnp.where(here, row, jnp.where(after, row_2, scaled))
            pivots = jnp.where(here, a, jnp.where(after, det * inv_a, pivots))
            for j in range(k + 2, SUBS):
                entry = over_subs(raw[k], j) * inv_a
                entry_2 = over_subs(plain, j) * a
                first = jnp.where(here, entry, corner[j] - corner[k] * entry)
                raw[j] = first - (second * entry_2) * inv_det
                corner[j] = jnp.where(after, entry_2 * inv_det, raw[j])
        result.append(scaled * jnp.sqrt(pivots))
        lead_rows = [over_subs(rows, k) for k in range(SUBS)]
        end = (s // per + 1) * per
        for t in range(s + 1, end):
            parts = [over_lanes(strips[t], base + k) * lead_rows[k] for k in range(SUBS)]
            while len(parts) > 1:
                parts = [x + y for x, y in zip(parts[::2], parts[1::2])]
            strips[t] = jnp.where(own, 0.0, strips[t]) - parts[0]
        if s + 1 == end < count:
            solved = jnp.concatenate(result, axis=0)
            lanes = lax.broadcasted_iota(jnp.int32, solved.shape, 1)
            subs = lax.broadcasted_iota(jnp.int32, solved.shape, 0)
            clean = jnp.where((lanes < SUBS * end) & (lanes > subs), 0.0, solved)
            change = lax.dot_general(
                solved,
                clean,
                (((0,), (0,)), ((), ())),
                precision=lax.Precision.HIGHEST,
                preferred_element_type=jnp.float32,
            )
            for t in range(end, count):
                keep = jnp.where(lane < SUBS * end, 0.0, strips[t])
                strips[t] = keep - change[SUBS * t : SUBS * (t + 1), :]
    result = [jnp.where(lane - SUBS * s <= sub, result[s], 0.0) for s in range(count)]
    return jnp.concatenate(result, axis=0)


def as_column(row):
    return jnp.broadcast_to(row, (LANES, LANES)).T


def reversed_bits(value, bits):
    out = 0
    for k in range(bits):
        out = out | (((value >> k) & 1) << (bits - 1 - k))
    return out


def bits_of(count):
    return count.bit_length() - 1


def kernel(*refs, ray_dev, row_count, col_count, lead, tops):
    near, near_x = refs[:2]
    lists = [refs[2 + k * tops : 2 + (k + 1) * tops] for k in range(4)]
    side, side_x, core, core_x = lists
    front, factor, feat, slot, noise, ray, mat, upper, lowers = refs[2 + 4 * tops :]
    row_index, col_index = lax.axis_index("row"), lax.axis_index("col")
    rows = ray_dev * col_count
    pair_count = near.shape[0]
    lead_pairs = lead // rows // 2
    cols = (pair_count - lead_pairs) * 2 * ray_dev
    row_pair, odd_row = row_index // 2, row_index % 2
    col_pair, odd_col = col_index // 2, col_index % 2
    lanes = lax.broadcasted_iota(jnp.int32, (1, LANES), 1)

    def aux_of(block):
        line = block[ray_dev : ray_dev + SUBS, :].astype(jnp.float32)[0:1]
        parts = [line[:, LANES * k : LANES * (k + 1)] for k in range(4)]
        return parts[0], parts[1] + parts[2] + parts[3]

    def put(mine, other, odd, to, numbers):
        here = pl.multiple_of(to + odd * ray_dev, ray_dev)
        there = pl.multiple_of(to + (1 - odd) * ray_dev, ray_dev)
        feat[pl.ds(here, ray_dev), :] = mine[:ray_dev, :]
        feat[pl.ds(there, ray_dev), :] = other[:ray_dev, :]
        tile = to // LANES
        for out, a, b in zip((slot, noise), aux_of(mine), aux_of(other)):
            even, late = jnp.where(odd == 0, a, b), jnp.where(odd == 0, b, a)
            out[pl.ds(tile, 1), :] = even + pltpu.roll(late, ray_dev, 1)
        ray[pl.ds(tile, 1), :] = numbers.astype(jnp.float32)

    low_bits = bits_of(lead_pairs)
    for k in range(lead_pairs):
        pair = (row_pair % lead_pairs) ^ reversed_bits(k, low_bits)
        for bit in range(2):
            row = pair * 2 + (odd_row if bit == 0 else 1 - odd_row)
            for top in range(tops):
                at = (col_pair ^ reversed_bits(top, bits_of(tops))) * LANES + row * rows
                mine, other = (side, core) if bit == 0 else (side_x, core_x)
                put(mine[top][k], other[top][k], odd_col, at, lanes + at)
    for top in range(tops):
        at = (col_pair ^ reversed_bits(top, bits_of(tops))) * LANES
        numbers = lanes + (row_index * rows + at)
        put(side[top][lead_pairs], core[top][lead_pairs], odd_col, lead + at, numbers)
    for place in range(pair_count):
        pair = row_pair ^ reversed_bits(place, bits_of(pair_count))

        @pl.when(pair >= lead_pairs)
        def _():
            numbers = ((pair * 2 + lanes // ray_dev) * col_count + col_index) * ray_dev
            numbers = numbers + lanes % ray_dev
            at = lead + rows + (pair - lead_pairs) * LANES
            put(near[place], near_x[place], odd_row, at, numbers)

    if cols % PANEL:
        feat[lead + rows + cols :, :] = jnp.zeros((PANEL - cols % PANEL, feat.shape[1]), feat.dtype)
        for out in (slot, noise, ray):
            out[(lead + rows + cols) // LANES :, :] = jnp.full((1, LANES), -1.0, jnp.float32)

    panels, row_tiles = lead // PANEL, rows // PANEL
    col_tiles = (cols + PANEL - 1) // PANEL

    def tile(i):
        start = i * PANEL
        return pl.ds(start if isinstance(start, int) else pl.multiple_of(start, PANEL), PANEL)

    def each(start, count, body):
        if count <= 2:
            for i in range(start, start + count):
                body(i)
        else:

            @pl.loop(start, start + count)
            def _(i):
                body(i)

    def column(source, i):
        return jnp.concatenate([as_column(source[pl.ds(2 * i + k, 1), :]) for k in range(2)], axis=0)

    def line(source, i):
        return [source[pl.ds(2 * i + k, 1), :] for k in range(2)]

    def fill(i, j, slot_a, ray_a=None):
        at = j if isinstance(j, int) and j < panels else j + row_tiles
        gram = lax.dot_general(
            feat[tile(i), :],
            feat[tile(at), :],
            (((1,), (1,)), ((), ())),
            preferred_element_type=jnp.float32,
        )
        halves = []
        for k, (slot_b, noise_b, ray_b) in enumerate(
            zip(line(slot, at), line(noise, at), line(ray, at))
        ):
            gap = slot_a - slot_b
            part = gram[:, k * LANES : (k + 1) * LANES] * jnp.exp(-gap * gap * time_rate())
            if ray_a is not None:
                part = part + jnp.where(ray_a == ray_b, noise_b, 0.0)
            halves.append(part)
        mat[tile(i), tile(j)] = jnp.concatenate(halves, axis=1)

    for i in range(panels):
        slot_a = column(slot, i)
        fill(i, i, slot_a, column(ray, i))
        for j in range(i + 1, panels):
            fill(i, j, slot_a)
        each(panels, col_tiles, lambda j: fill(i, j, slot_a))

    def fill_row(i):
        slot_a, ray_a = column(slot, i), column(ray, i)
        for j in range(panels):
            fill(i, j, slot_a, ray_a)
        each(panels, col_tiles, lambda j: fill(i, j, slot_a, ray_a))

    each(panels, row_tiles, fill_row)

    for p in range(panels):
        at = p * PANEL
        mid = at + HALF
        inv_a = inverse_factor(mat[at:mid, at:mid])
        cross = product(left(inv_a), right(mat[at:mid, mid : mid + HALF]))
        cross_left, cross_right = left(cross.T), right(cross)
        corner = mat[mid : mid + HALF, mid : mid + HALF] - product(cross_left, cross_right)
        inv_b = inverse_factor(corner)
        below = product(left(-inv_b), right(product(cross_left, right(inv_a))))
        zero = jnp.zeros((HALF, HALF), jnp.float32)
        inv = jnp.concatenate(
            [jnp.concatenate([inv_a, zero], axis=1), jnp.concatenate([below, inv_b], axis=1)], axis=0
        )
        inv_left, inv_right = left(inv), right(inv.T)

        def solve(j):
            found = product(inv_left, right(mat[tile(p), tile(j)]))
            upper[:, tile(j)] = right(found)
            return found

        def update(i, j, lower):
            mat[tile(i), tile(j)] -= product(lower, upper[:, tile(j)])

        for j in range(p + 1, panels):
            lowers[tile(j), :] = left(solve(j).T)
            update(j, j, lowers[tile(j), :])
        each(panels, col_tiles, solve)
        for q in range(p + 1, panels):
            for j in range(q + 1, panels):
                update(q, j, lowers[tile(q), :])
            each(panels, col_tiles, lambda j: update(q, j, lowers[tile(q), :]))

        def solve_row(i):
            found = product(left(mat[tile(panels + i), tile(p)]), inv_right)
            ray_a = column(ray, panels + i)
            kept = [
                jnp.where(ray_a >= ray_b, found[:, k * LANES : (k + 1) * LANES], 0.0)
                for k, ray_b in enumerate(line(ray, p))
            ]
            factor[tile(i), tile(p)] = jnp.concatenate(kept, axis=1)
            lower = left(found)
            for j in range(p + 1, panels):
                update(panels + i, j, lower)
            each(panels, col_tiles, lambda j: update(panels + i, j, lower))

        each(0, row_tiles, solve_row)

    skipped = front.shape[1] - cols
    front[:, 0:skipped] = jnp.zeros((rows, skipped), jnp.float32)
    front[:, skipped:] = jnp.where(
        row_index * rows >= lead, mat[lead : lead + rows, lead : lead + cols], 0.0
    )


def packed(features, slot_of_ray, noise):
    high = lax.reduce_precision(noise, 8, 7)
    middle = lax.reduce_precision(noise - high, 8, 7)
    terms = jnp.stack([slot_of_ray.astype(jnp.float32), high, middle, noise - high - middle])
    ray_dev, width = features.shape
    aux = jnp.pad(terms, ((0, 0), (0, LANES - ray_dev))).reshape(1, 4 * LANES)
    aux = jnp.pad(aux, ((0, SUBS - 1), (0, width - 4 * LANES))).astype(features.dtype)
    return jnp.concatenate([features, aux])


def shards(features, slot_of_ray, noise):
    ray_dev = noise.shape[0]
    row_count, col_count = lax.axis_size("row"), lax.axis_size("col")
    rows, col_width = ray_dev * col_count, ray_dev * row_count
    row_index = lax.axis_index("row")
    lead = PANELS * PANEL
    row_bits, col_bits = bits_of(row_count), bits_of(col_count)
    tops = col_count // 2
    lead_pairs = lead // rows // 2

    def other(value, axis, bit):
        count = lax.axis_size(axis)
        return lax.ppermute(value, axis, [(k, k ^ (1 << bit)) for k in range(count)])

    near = packed(features, slot_of_ray, noise)[None]
    own = near
    for bit in reversed(range(1, row_bits)):
        near = jnp.concatenate([near, other(near, "row", bit)])
    high_bits = row_bits - 1 - bits_of(lead_pairs)
    group = reversed_bits(row_index >> (row_bits - high_bits), high_bits)

    def leading(blocks):
        split = blocks.reshape(lead_pairs, 1 << high_bits, *blocks.shape[1:])
        return lax.dynamic_index_in_dim(split, group, 1, False)

    near_x = other(near, "row", 0)
    side = [jnp.concatenate([leading(near), own])]
    side_x = [leading(near_x)]
    for bit in reversed(range(1, col_bits)):
        side += [other(value, "col", bit) for value in side]
        side_x += [other(value, "col", bit) for value in side_x]
    core = [other(value, "col", 0) for value in side]
    core_x = [other(value, "col", 0) for value in side_x]

    cols = col_width - lead // col_count
    padded = -(-cols // PANEL) * PANEL
    rays = lead + rows + padded
    front, factor = pl.pallas_call(
        functools.partial(
            kernel, ray_dev=ray_dev, row_count=row_count, col_count=col_count, lead=lead, tops=tops
        ),
        out_shape=(
            jax.ShapeDtypeStruct((rows, col_width), jnp.float32),
            jax.ShapeDtypeStruct((rows, lead), jnp.float32),
        ),
        scratch_shapes=[
            pltpu.VMEM((rays, features.shape[1]), features.dtype),
            *[pltpu.VMEM((rays // LANES, LANES), jnp.float32)] * 3,
            pltpu.VMEM((lead + rows, lead + padded), jnp.float32),
            pltpu.VMEM((6 * PANEL, lead + padded), jnp.bfloat16),
            pltpu.VMEM((lead, 6 * PANEL), jnp.bfloat16),
        ],
        name="panels",
    )(near, near_x, *side, *side_x, *core, *core_x)
    return front.reshape(rows, 1, col_width), factor


def solution(mesh):
    return jax.shard_map(
        shards,
        mesh=mesh,
        in_specs=(P(("row", "col"), None), P(("row", "col")), P(("row", "col"))),
        out_specs=(P("row", "col", None), P("row", None)),
        check_vma=False,
    )
```

```python
import functools

import jax
import jax.numpy as jnp
from jax import lax
from jax.experimental import pallas as pl
from jax.experimental.pallas import tpu as pltpu
from jax.sharding import PartitionSpec as P

PANEL = 256
PANELS = 4
NT = 64
LANES = 128
SUBS = 8
HALF = PANEL // 2


def time_rate():
    length = NT / 8.0
    return 1.0 / (2.0 * length * length)


def terms_of(value):
    high = value.astype(jnp.bfloat16)
    rest = value - high.astype(jnp.float32)
    middle = rest.astype(jnp.bfloat16)
    low = (rest - middle.astype(jnp.float32)).astype(jnp.bfloat16)
    return high, middle, low


def left(value):
    high, middle, low = terms_of(value)
    return jnp.concatenate([low, high, middle, middle, high, high], axis=1)


def right(value):
    high, middle, low = terms_of(value)
    return jnp.concatenate([high, low, middle, high, middle, high], axis=0)


def product(a, b):
    return jnp.dot(a, b, preferred_element_type=jnp.float32)


def inverse_factor(block):
    count = block.shape[0] // SUBS
    per, ahead = count // 2, SUBS // 2
    strips = [block[SUBS * t : SUBS * (t + 1), :] for t in range(count)]
    shape = (SUBS, LANES)
    lane = lax.broadcasted_iota(jnp.int32, shape, 1)
    sub = lax.broadcasted_iota(jnp.int32, shape, 0)

    def over_subs(x, k):
        return jnp.broadcast_to(x[k : k + 1, :], shape)

    def over_lanes(x, j):
        return jnp.broadcast_to(x[:, j : j + 1], shape)

    result = []
    early = []
    for s in range(count):
        base = SUBS * s
        end = (s // per + 1) * per
        raw = early + [over_lanes(strips[s], base + j) for j in range(len(early), SUBS)]
        corner = list(raw)
        own = (lane >= base) & (lane < base + SUBS)
        rows = jnp.where(own, jnp.where(lane - base == sub, 1.0, 0.0), strips[s])
        scaled = rows
        pivots = rows
        near = s + 1 < end
        early = []
        if near:
            cols = [over_lanes(strips[s + 1], base + k) for k in range(SUBS)]
            early = [over_lanes(strips[s + 1], base + SUBS + j) for j in range(ahead)]
            following = jnp.where(own, 0.0, strips[s + 1])
        for k in range(0, SUBS, 2):
            here, after = sub == k, sub == k + 1
            a, b, c = over_subs(raw[k], k), over_subs(raw[k], k + 1), over_subs(raw[k + 1], k + 1)
            det = a * c - b * b
            inv_a, inv_det = 1.0 / a, 1.0 / det
            ratio = b * inv_a
            plain = corner[k + 1] - corner[k] * ratio
            second = jnp.where(here, ratio, plain)
            row = over_subs(rows, k) * inv_a
            rows = jnp.where(here, row, rows - corner[k] * row)
            row_2 = (over_subs(rows, k + 1) * a) * inv_det
            rows = jnp.where(after, row_2, rows - second * row_2)
            scaled = jnp.where(here, row, jnp.where(after, row_2, scaled))
            pivots = jnp.where(here, a, jnp.where(after, det * inv_a, pivots))
            entries = []
            for j in range(k + 2, SUBS):
                entry = over_subs(raw[k], j) * inv_a
                entry_2 = over_subs(plain, j) * a
                entries.append((entry, entry_2))
                first = jnp.where(here, entry, corner[j] - corner[k] * entry)
                raw[j] = first - (second * entry_2) * inv_det
                corner[j] = jnp.where(after, entry_2 * inv_det, raw[j])
            if near:
                col = cols[k]
                col_2 = cols[k + 1] - col * ratio
                for j, (entry, entry_2) in zip(range(k + 2, SUBS), entries):
                    cols[j] = (cols[j] - col * entry) - (col_2 * entry_2) * inv_det
                following = (following - col * row) - col_2 * row_2
                for j in range(ahead):
                    part = early[j] - col * (over_subs(col, j) * inv_a)
                    early[j] = part - (col_2 * (over_subs(col_2, j) * a)) * inv_det
        result.append(scaled * jnp.sqrt(pivots))
        if near:
            strips[s + 1] = following
        if s + 2 < end:
            lead_rows = [over_subs(rows, k) for k in range(SUBS)]
        for t in range(s + 2, end):
            parts = [over_lanes(strips[t], base + k) * lead_rows[k] for k in range(SUBS)]
            while len(parts) > 1:
                parts = [x + y for x, y in zip(parts[::2], parts[1::2])]
            strips[t] = jnp.where(own, 0.0, strips[t]) - parts[0]
        if s + 1 == end < count:
            solved = jnp.concatenate(result, axis=0)
            lanes = lax.broadcasted_iota(jnp.int32, solved.shape, 1)
            subs = lax.broadcasted_iota(jnp.int32, solved.shape, 0)
            clean = jnp.where((lanes < SUBS * end) & (lanes > subs), 0.0, solved)
            change = lax.dot_general(
                solved,
                clean,
                (((0,), (0,)), ((), ())),
                precision=lax.Precision.HIGHEST,
                preferred_element_type=jnp.float32,
            )
            for t in range(end, count):
                keep = jnp.where(lane < SUBS * end, 0.0, strips[t])
                strips[t] = keep - change[SUBS * t : SUBS * (t + 1), :]
    result = [jnp.where(lane - SUBS * s <= sub, result[s], 0.0) for s in range(count)]
    return jnp.concatenate(result, axis=0)


def as_column(row):
    return jnp.broadcast_to(row, (LANES, LANES)).T


def reversed_bits(value, bits):
    out = 0
    for k in range(bits):
        out = out | (((value >> k) & 1) << (bits - 1 - k))
    return out


def bits_of(count):
    return count.bit_length() - 1


def kernel(*refs, ray_dev, row_count, col_count, lead, tops):
    near, near_x = refs[:2]
    lists = [refs[2 + k * tops : 2 + (k + 1) * tops] for k in range(4)]
    side, side_x, core, core_x = lists
    front, factor, feat, slot, noise, ray, mat, upper, lowers = refs[2 + 4 * tops :]
    row_index, col_index = lax.axis_index("row"), lax.axis_index("col")
    rows = ray_dev * col_count
    pair_count = near.shape[0]
    lead_pairs = lead // rows // 2
    cols = (pair_count - lead_pairs) * 2 * ray_dev
    row_pair, odd_row = row_index // 2, row_index % 2
    col_pair, odd_col = col_index // 2, col_index % 2
    lanes = lax.broadcasted_iota(jnp.int32, (1, LANES), 1)

    def aux_of(block):
        line = block[ray_dev : ray_dev + SUBS, :].astype(jnp.float32)[0:1]
        parts = [line[:, LANES * k : LANES * (k + 1)] for k in range(4)]
        return parts[0], parts[1] + parts[2] + parts[3]

    def put(mine, other, odd, to, numbers):
        here = pl.multiple_of(to + odd * ray_dev, ray_dev)
        there = pl.multiple_of(to + (1 - odd) * ray_dev, ray_dev)
        feat[pl.ds(here, ray_dev), :] = mine[:ray_dev, :]
        feat[pl.ds(there, ray_dev), :] = other[:ray_dev, :]
        tile = to // LANES
        for out, a, b in zip((slot, noise), aux_of(mine), aux_of(other)):
            even, late = jnp.where(odd == 0, a, b), jnp.where(odd == 0, b, a)
            out[pl.ds(tile, 1), :] = even + pltpu.roll(late, ray_dev, 1)
        ray[pl.ds(tile, 1), :] = numbers.astype(jnp.float32)

    low_bits = bits_of(lead_pairs)
    for k in range(lead_pairs):
        pair = (row_pair % lead_pairs) ^ reversed_bits(k, low_bits)
        for bit in range(2):
            row = pair * 2 + (odd_row if bit == 0 else 1 - odd_row)
            for top in range(tops):
                at = (col_pair ^ reversed_bits(top, bits_of(tops))) * LANES + row * rows
                mine, other = (side, core) if bit == 0 else (side_x, core_x)
                put(mine[top][k], other[top][k], odd_col, at, lanes + at)
    for top in range(tops):
        at = (col_pair ^ reversed_bits(top, bits_of(tops))) * LANES
        numbers = lanes + (row_index * rows + at)
        put(side[top][lead_pairs], core[top][lead_pairs], odd_col, lead + at, numbers)
    for place in range(pair_count):
        pair = row_pair ^ reversed_bits(place, bits_of(pair_count))

        @pl.when(pair >= lead_pairs)
        def _():
            numbers = ((pair * 2 + lanes // ray_dev) * col_count + col_index) * ray_dev
            numbers = numbers + lanes % ray_dev
            at = lead + rows + (pair - lead_pairs) * LANES
            put(near[place], near_x[place], odd_row, at, numbers)

    if cols % PANEL:
        feat[lead + rows + cols :, :] = jnp.zeros((PANEL - cols % PANEL, feat.shape[1]), feat.dtype)
        for out in (slot, noise, ray):
            out[(lead + rows + cols) // LANES :, :] = jnp.full((1, LANES), -1.0, jnp.float32)

    panels, row_tiles = lead // PANEL, rows // PANEL
    col_tiles = (cols + PANEL - 1) // PANEL

    def tile(i):
        start = i * PANEL
        return pl.ds(start if isinstance(start, int) else pl.multiple_of(start, PANEL), PANEL)

    def each(start, count, body):
        if count <= 2:
            for i in range(start, start + count):
                body(i)
        else:

            @pl.loop(start, start + count)
            def _(i):
                body(i)

    def column(source, i):
        return jnp.concatenate([as_column(source[pl.ds(2 * i + k, 1), :]) for k in range(2)], axis=0)

    def line(source, i):
        return [source[pl.ds(2 * i + k, 1), :] for k in range(2)]

    def fill(i, j, slot_a, ray_a=None):
        at = j if isinstance(j, int) and j < panels else j + row_tiles
        gram = lax.dot_general(
            feat[tile(i), :],
            feat[tile(at), :],
            (((1,), (1,)), ((), ())),
            preferred_element_type=jnp.float32,
        )
        halves = []
        for k, (slot_b, noise_b, ray_b) in enumerate(
            zip(line(slot, at), line(noise, at), line(ray, at))
        ):
            gap = slot_a - slot_b
            part = gram[:, k * LANES : (k + 1) * LANES] * jnp.exp(-gap * gap * time_rate())
            if ray_a is not None:
                part = part + jnp.where(ray_a == ray_b, noise_b, 0.0)
            halves.append(part)
        mat[tile(i), tile(j)] = jnp.concatenate(halves, axis=1)

    for i in range(panels):
        slot_a = column(slot, i)
        fill(i, i, slot_a, column(ray, i))
        for j in range(i + 1, panels):
            fill(i, j, slot_a)
        each(panels, col_tiles, lambda j: fill(i, j, slot_a))

    def fill_row(i):
        slot_a, ray_a = column(slot, i), column(ray, i)
        for j in range(panels):
            fill(i, j, slot_a, ray_a)
        each(panels, col_tiles, lambda j: fill(i, j, slot_a, ray_a))

    each(panels, row_tiles, fill_row)

    half = 6 * HALF

    for p in range(panels):
        top, low = pl.ds(p * PANEL, HALF), pl.ds(p * PANEL + HALF, HALF)
        inv_a = inverse_factor(mat[top, top])
        left_a = left(inv_a)
        cross = product(left_a, right(mat[top, low]))
        cross_left, cross_right = left(cross.T), right(cross)
        corner = mat[low, low] - product(cross_left, cross_right)

        def solve_top(j):
            found = product(left_a, right(mat[top, tile(j)]))
            terms = right(found)
            upper[0:half, tile(j)] = terms
            mat[low, tile(j)] -= product(cross_left, terms)
            return found

        def solve_low(j):
            found = product(left_b, right(mat[low, tile(j)]))
            upper[half:, tile(j)] = right(found)
            return found

        for j in range(p + 1, panels):
            lowers[tile(j), 0:half] = left(solve_top(j).T)
        if p + 1 < panels:
            mat[tile(p + 1), tile(p + 1)] -= product(
                lowers[tile(p + 1), 0:half], upper[0:half, tile(p + 1)]
            )
        inv_b = inverse_factor(corner)
        left_b = left(inv_b)
        for j in range(p + 1, panels):
            lowers[tile(j), half:] = left(solve_low(j).T)
            if j == p + 1:
                mat[tile(j), tile(j)] -= product(lowers[tile(j), half:], upper[half:, tile(j)])

        def solve(j):
            solve_top(j)
            solve_low(j)

        each(panels, col_tiles, solve)
        right_a, right_b = right(inv_a.T), right(inv_b.T)

        def solve_row(i):
            row = tile(panels + i)
            first = product(left(mat[row, top]), right_a)
            first_left = left(first)
            second = product(left(mat[row, low] - product(first_left, cross_right)), right_b)
            ray_a = column(ray, panels + i)
            kept = [
                jnp.where(ray_a >= ray_b, part, 0.0)
                for part, ray_b in zip((first, second), line(ray, p))
            ]
            factor[tile(i), tile(p)] = jnp.concatenate(kept, axis=1)
            lowers[row, 0:half] = first_left
            lowers[row, half:] = left(second)

        each(0, row_tiles, solve_row)

        def update(start, count, j):
            some = pl.ds(start * PANEL, count * PANEL)
            mat[some, tile(j)] -= product(lowers[some, :], upper[:, tile(j)])

        for j in range(p + 1, panels):
            if j > p + 1:
                update(p + 1, j - p, j)
            update(panels, row_tiles, j)
        each(panels, col_tiles, lambda j: update(p + 1, panels + row_tiles - p - 1, j))

    skipped = front.shape[1] - cols
    front[:, 0:skipped] = jnp.zeros((rows, skipped), jnp.float32)
    front[:, skipped:] = jnp.where(
        row_index * rows >= lead, mat[lead : lead + rows, lead : lead + cols], 0.0
    )


def packed(features, slot_of_ray, noise):
    high = lax.reduce_precision(noise, 8, 7)
    middle = lax.reduce_precision(noise - high, 8, 7)
    terms = jnp.stack([slot_of_ray.astype(jnp.float32), high, middle, noise - high - middle])
    ray_dev, width = features.shape
    aux = jnp.pad(terms, ((0, 0), (0, LANES - ray_dev))).reshape(1, 4 * LANES)
    aux = jnp.pad(aux, ((0, SUBS - 1), (0, width - 4 * LANES))).astype(features.dtype)
    return jnp.concatenate([features, aux])


def shards(features, slot_of_ray, noise):
    ray_dev = noise.shape[0]
    row_count, col_count = lax.axis_size("row"), lax.axis_size("col")
    rows, col_width = ray_dev * col_count, ray_dev * row_count
    row_index = lax.axis_index("row")
    lead = PANELS * PANEL
    row_bits, col_bits = bits_of(row_count), bits_of(col_count)
    tops = col_count // 2
    lead_pairs = lead // rows // 2

    def other(value, axis, bit):
        count = lax.axis_size(axis)
        return lax.ppermute(value, axis, [(k, k ^ (1 << bit)) for k in range(count)])

    near = packed(features, slot_of_ray, noise)[None]
    own = near
    for bit in reversed(range(1, row_bits)):
        near = jnp.concatenate([near, other(near, "row", bit)])
    high_bits = row_bits - 1 - bits_of(lead_pairs)
    group = reversed_bits(row_index >> (row_bits - high_bits), high_bits)

    def leading(blocks):
        split = blocks.reshape(lead_pairs, 1 << high_bits, *blocks.shape[1:])
        return lax.dynamic_index_in_dim(split, group, 1, False)

    near_x = other(near, "row", 0)
    side = [jnp.concatenate([leading(near), own])]
    side_x = [leading(near_x)]
    for bit in reversed(range(1, col_bits)):
        side += [other(value, "col", bit) for value in side]
        side_x += [other(value, "col", bit) for value in side_x]
    core = [other(value, "col", 0) for value in side]
    core_x = [other(value, "col", 0) for value in side_x]

    cols = col_width - lead // col_count
    padded = -(-cols // PANEL) * PANEL
    rays = lead + rows + padded
    front, factor = pl.pallas_call(
        functools.partial(
            kernel, ray_dev=ray_dev, row_count=row_count, col_count=col_count, lead=lead, tops=tops
        ),
        out_shape=(
            jax.ShapeDtypeStruct((rows, col_width), jnp.float32),
            jax.ShapeDtypeStruct((rows, lead), jnp.float32),
        ),
        scratch_shapes=[
            pltpu.VMEM((rays, features.shape[1]), features.dtype),
            *[pltpu.VMEM((rays // LANES, LANES), jnp.float32)] * 3,
            pltpu.VMEM((lead + rows, lead + padded), jnp.float32),
            pltpu.VMEM((6 * PANEL, lead + padded), jnp.bfloat16),
            pltpu.VMEM((lead + rows, 6 * PANEL), jnp.bfloat16),
        ],
        name="panels",
    )(near, near_x, *side, *side_x, *core, *core_x)
    return front.reshape(rows, 1, col_width), factor


def solution(mesh):
    return jax.shard_map(
        shards,
        mesh=mesh,
        in_specs=(P(("row", "col"), None), P(("row", "col")), P(("row", "col"))),
        out_specs=(P("row", "col", None), P("row", None)),
        check_vma=False,
    )
```

```python
import functools

import jax
import jax.numpy as jnp
from jax import lax
from jax.experimental import pallas as pl
from jax.experimental.pallas import tpu as pltpu
from jax.sharding import PartitionSpec as P

PANEL = 256
PANELS = 4
NT = 64
LANES = 128
SUBS = 8
HALF = PANEL // 2


def time_rate():
    length = NT / 8.0
    return 1.0 / (2.0 * length * length)


def terms_of(value):
    high = value.astype(jnp.bfloat16)
    rest = value - high.astype(jnp.float32)
    middle = rest.astype(jnp.bfloat16)
    low = (rest - middle.astype(jnp.float32)).astype(jnp.bfloat16)
    return high, middle, low


def left(value):
    high, middle, low = terms_of(value)
    return jnp.concatenate([low, high, middle, middle, high, high], axis=1)


def right(value):
    high, middle, low = terms_of(value)
    return jnp.concatenate([high, low, middle, high, middle, high], axis=0)


def product(a, b):
    return jnp.dot(a, b, preferred_element_type=jnp.float32)


def inverse_factor(block):
    count = block.shape[0] // SUBS
    per, ahead = count // 2, SUBS // 2
    strips = [block[SUBS * t : SUBS * (t + 1), :] for t in range(count)]
    shape = (SUBS, LANES)
    lane = lax.broadcasted_iota(jnp.int32, shape, 1)
    sub = lax.broadcasted_iota(jnp.int32, shape, 0)

    def over_subs(x, k):
        return jnp.broadcast_to(x[k : k + 1, :], shape)

    def over_lanes(x, j):
        return jnp.broadcast_to(x[:, j : j + 1], shape)

    result = []
    early = []
    for s in range(count):
        base = SUBS * s
        end = (s // per + 1) * per
        raw = early + [over_lanes(strips[s], base + j) for j in range(len(early), SUBS)]
        corner = list(raw)
        own = (lane >= base) & (lane < base + SUBS)
        rows = jnp.where(own, jnp.where(lane - base == sub, 1.0, 0.0), strips[s])
        scaled = rows
        pivots = rows
        near = s + 1 < end
        early = []
        if near:
            cols = [over_lanes(strips[s + 1], base + k) for k in range(SUBS)]
            early = [over_lanes(strips[s + 1], base + SUBS + j) for j in range(ahead)]
            following = jnp.where(own, 0.0, strips[s + 1])
        for k in range(0, SUBS, 2):
            here, after = sub == k, sub == k + 1
            a, b, c = over_subs(raw[k], k), over_subs(raw[k], k + 1), over_subs(raw[k + 1], k + 1)
            det = a * c - b * b
            inv_a, inv_det = 1.0 / a, 1.0 / det
            ratio = b * inv_a
            plain = corner[k + 1] - corner[k] * ratio
            second = jnp.where(here, ratio, plain)
            row = over_subs(rows, k) * inv_a
            rows = jnp.where(here, row, rows - corner[k] * row)
            row_2 = (over_subs(rows, k + 1) * a) * inv_det
            rows = jnp.where(after, row_2, rows - second * row_2)
            scaled = jnp.where(here, row, jnp.where(after, row_2, scaled))
            pivots = jnp.where(here, a, jnp.where(after, det * inv_a, pivots))
            entries = []
            for j in range(k + 2, SUBS):
                entry = over_subs(raw[k], j) * inv_a
                entry_2 = over_subs(plain, j) * a
                entries.append((entry, entry_2))
                first = jnp.where(here, entry, corner[j] - corner[k] * entry)
                raw[j] = first - (second * entry_2) * inv_det
                corner[j] = jnp.where(after, entry_2 * inv_det, raw[j])
            if near:
                col = cols[k]
                col_2 = cols[k + 1] - col * ratio
                for j, (entry, entry_2) in zip(range(k + 2, SUBS), entries):
                    cols[j] = (cols[j] - col * entry) - (col_2 * entry_2) * inv_det
                following = (following - col * row) - col_2 * row_2
                for j in range(ahead):
                    part = early[j] - col * (over_subs(col, j) * inv_a)
                    early[j] = part - (col_2 * (over_subs(col_2, j) * a)) * inv_det
        result.append(scaled * jnp.sqrt(pivots))
        if near:
            strips[s + 1] = following
        if s + 2 < end:
            lead_rows = [over_subs(rows, k) for k in range(SUBS)]
        for t in range(s + 2, end):
            parts = [over_lanes(strips[t], base + k) * lead_rows[k] for k in range(SUBS)]
            while len(parts) > 1:
                parts = [x + y for x, y in zip(parts[::2], parts[1::2])]
            strips[t] = jnp.where(own, 0.0, strips[t]) - parts[0]
        if s + 1 == end < count:
            solved = jnp.concatenate(result, axis=0)
            lanes = lax.broadcasted_iota(jnp.int32, solved.shape, 1)
            subs = lax.broadcasted_iota(jnp.int32, solved.shape, 0)
            clean = jnp.where((lanes < SUBS * end) & (lanes > subs), 0.0, solved)
            change = lax.dot_general(
                solved,
                clean,
                (((0,), (0,)), ((), ())),
                precision=lax.Precision.HIGHEST,
                preferred_element_type=jnp.float32,
            )
            for t in range(end, count):
                keep = jnp.where(lane < SUBS * end, 0.0, strips[t])
                strips[t] = keep - change[SUBS * t : SUBS * (t + 1), :]
    result = [jnp.where(lane - SUBS * s <= sub, result[s], 0.0) for s in range(count)]
    return jnp.concatenate(result, axis=0)


def as_column(row):
    return jnp.broadcast_to(row, (LANES, LANES)).T


def reversed_bits(value, bits):
    out = 0
    for k in range(bits):
        out = out | (((value >> k) & 1) << (bits - 1 - k))
    return out


def bits_of(count):
    return count.bit_length() - 1


def kernel(*refs, ray_dev, row_count, col_count, lead, tops):
    near, near_x = refs[:2]
    lists = [refs[2 + k * tops : 2 + (k + 1) * tops] for k in range(4)]
    side, side_x, core, core_x = lists
    front, factor, feat, slot, noise, ray, mat, upper, lowers = refs[2 + 4 * tops :]
    row_index, col_index = lax.axis_index("row"), lax.axis_index("col")
    rows = ray_dev * col_count
    pair_count = near.shape[0]
    lead_pairs = lead // rows // 2
    cols = (pair_count - lead_pairs) * 2 * ray_dev
    row_pair, odd_row = row_index // 2, row_index % 2
    col_pair, odd_col = col_index // 2, col_index % 2
    lanes = lax.broadcasted_iota(jnp.int32, (1, LANES), 1)

    def aux_of(block):
        lines = block[ray_dev : ray_dev + SUBS, 0:LANES].astype(jnp.float32)
        parts = [lines[k : k + 1] for k in range(4)]
        return parts[0], parts[1] + parts[2] + parts[3]

    def put(mine, other, odd, to, numbers):
        here = pl.multiple_of(to + odd * ray_dev, ray_dev)
        there = pl.multiple_of(to + (1 - odd) * ray_dev, ray_dev)
        feat[pl.ds(here, ray_dev), :] = mine[:ray_dev, :]
        feat[pl.ds(there, ray_dev), :] = other[:ray_dev, :]
        tile = to // LANES
        for out, a, b in zip((slot, noise), aux_of(mine), aux_of(other)):
            even, late = jnp.where(odd == 0, a, b), jnp.where(odd == 0, b, a)
            out[pl.ds(tile, 1), :] = even + pltpu.roll(late, ray_dev, 1)
        ray[pl.ds(tile, 1), :] = numbers.astype(jnp.float32)

    low_bits = bits_of(lead_pairs)
    for k in range(lead_pairs):
        pair = (row_pair % lead_pairs) ^ reversed_bits(k, low_bits)
        for bit in range(2):
            row = pair * 2 + (odd_row if bit == 0 else 1 - odd_row)
            for top in range(tops):
                at = (col_pair ^ reversed_bits(top, bits_of(tops))) * LANES + row * rows
                mine, other = (side, core) if bit == 0 else (side_x, core_x)
                put(mine[top][k], other[top][k], odd_col, at, lanes + at)
    for top in range(tops):
        at = (col_pair ^ reversed_bits(top, bits_of(tops))) * LANES
        numbers = lanes + (row_index * rows + at)
        put(side[top][lead_pairs], core[top][lead_pairs], odd_col, lead + at, numbers)
    for place in range(pair_count):
        pair = row_pair ^ reversed_bits(place, bits_of(pair_count))

        @pl.when(pair >= lead_pairs)
        def _():
            numbers = ((pair * 2 + lanes // ray_dev) * col_count + col_index) * ray_dev
            numbers = numbers + lanes % ray_dev
            at = lead + rows + (pair - lead_pairs) * LANES
            put(near[place], near_x[place], odd_row, at, numbers)

    if cols % PANEL:
        feat[lead + rows + cols :, :] = jnp.zeros((PANEL - cols % PANEL, feat.shape[1]), feat.dtype)
        for out in (slot, noise, ray):
            out[(lead + rows + cols) // LANES :, :] = jnp.full((1, LANES), -1.0, jnp.float32)

    panels, row_tiles = lead // PANEL, rows // PANEL
    col_tiles = (cols + PANEL - 1) // PANEL

    skipped = front.shape[2] - cols
    front[:, 0, 0:skipped] = jnp.zeros((rows, skipped), jnp.float32)

    def tile(i):
        start = i * PANEL
        return pl.ds(start if isinstance(start, int) else pl.multiple_of(start, PANEL), PANEL)

    def each(start, count, body):
        if count <= 2:
            for i in range(start, start + count):
                body(i)
        else:

            @pl.loop(start, start + count)
            def _(i):
                body(i)

    def column(source, i):
        return jnp.concatenate([as_column(source[pl.ds(2 * i + k, 1), :]) for k in range(2)], axis=0)

    def line(source, i):
        return [source[pl.ds(2 * i + k, 1), :] for k in range(2)]

    def fill(i, j, slot_a, ray_a=None):
        at = j if isinstance(j, int) and j < panels else j + row_tiles
        gram = lax.dot_general(
            feat[tile(i), :],
            feat[tile(at), :],
            (((1,), (1,)), ((), ())),
            preferred_element_type=jnp.float32,
        )
        halves = []
        for k, (slot_b, noise_b, ray_b) in enumerate(
            zip(line(slot, at), line(noise, at), line(ray, at))
        ):
            gap = slot_a - slot_b
            part = gram[:, k * LANES : (k + 1) * LANES] * jnp.exp(-gap * gap * time_rate())
            if ray_a is not None:
                part = part + jnp.where(ray_a == ray_b, noise_b, 0.0)
            halves.append(part)
        mat[tile(i), tile(j)] = jnp.concatenate(halves, axis=1)

    for i in range(panels):
        slot_a = column(slot, i)
        fill(i, i, slot_a, column(ray, i))
        for j in range(i + 1, panels):
            fill(i, j, slot_a)
        each(panels, col_tiles, lambda j: fill(i, j, slot_a))

    def fill_row(i):
        slot_a, ray_a = column(slot, i), column(ray, i)
        for j in range(panels):
            fill(i, j, slot_a, ray_a)
        each(panels, col_tiles, lambda j: fill(i, j, slot_a, ray_a))

    each(panels, row_tiles, fill_row)

    half = 6 * HALF

    for p in range(panels):
        top, low = pl.ds(p * PANEL, HALF), pl.ds(p * PANEL + HALF, HALF)
        inv_a = inverse_factor(mat[top, top])
        left_a = left(inv_a)
        cross = product(left_a, right(mat[top, low]))
        cross_left, cross_right = left(cross.T), right(cross)
        corner = mat[low, low] - product(cross_left, cross_right)

        def solve_top(j):
            found = product(left_a, right(mat[top, tile(j)]))
            terms = right(found)
            upper[0:half, tile(j)] = terms
            mat[low, tile(j)] -= product(cross_left, terms)
            return found

        def solve_low(j):
            found = product(left_b, right(mat[low, tile(j)]))
            upper[half:, tile(j)] = right(found)
            return found

        for j in range(p + 1, panels):
            lowers[tile(j), 0:half] = left(solve_top(j).T)
        if p + 1 < panels:
            mat[tile(p + 1), tile(p + 1)] -= product(
                lowers[tile(p + 1), 0:half], upper[0:half, tile(p + 1)]
            )
        inv_b = inverse_factor(corner)
        left_b = left(inv_b)
        for j in range(p + 1, panels):
            lowers[tile(j), half:] = left(solve_low(j).T)
            if j == p + 1:
                mat[tile(j), tile(j)] -= product(lowers[tile(j), half:], upper[half:, tile(j)])

        def solve(j):
            solve_top(j)
            solve_low(j)

        each(panels, col_tiles, solve)
        right_a, right_b = right(inv_a.T), right(inv_b.T)

        def solve_row(i):
            row = tile(panels + i)
            first = product(left(mat[row, top]), right_a)
            first_left = left(first)
            second = product(left(mat[row, low] - product(first_left, cross_right)), right_b)
            ray_a = column(ray, panels + i)
            kept = [
                jnp.where(ray_a >= ray_b, part, 0.0)
                for part, ray_b in zip((first, second), line(ray, p))
            ]
            factor[tile(i), tile(p)] = jnp.concatenate(kept, axis=1)
            lowers[row, 0:half] = first_left
            lowers[row, half:] = left(second)

        each(0, row_tiles, solve_row)

        def update(start, count, j):
            some = pl.ds(start * PANEL, count * PANEL)
            mat[some, tile(j)] -= product(lowers[some, :], upper[:, tile(j)])

        for j in range(p + 1, panels):
            if j > p + 1:
                update(p + 1, j - p, j)
            update(panels, row_tiles, j)
        each(panels, col_tiles, lambda j: update(p + 1, panels + row_tiles - p - 1, j))

    front[:, 0, skipped:] = jnp.where(
        row_index * rows >= lead, mat[lead : lead + rows, lead : lead + cols], 0.0
    )


def packed(features, slot_of_ray, noise):
    high = lax.reduce_precision(noise, 8, 7)
    middle = lax.reduce_precision(noise - high, 8, 7)
    terms = jnp.stack([slot_of_ray.astype(jnp.float32), high, middle, noise - high - middle])
    ray_dev, width = features.shape
    aux = jnp.pad(terms, ((0, SUBS - 4), (0, width - ray_dev))).astype(features.dtype)
    return jnp.concatenate([features, aux])


def shards(features, slot_of_ray, noise):
    ray_dev = noise.shape[0]
    row_count, col_count = lax.axis_size("row"), lax.axis_size("col")
    rows, col_width = ray_dev * col_count, ray_dev * row_count
    row_index = lax.axis_index("row")
    lead = PANELS * PANEL
    row_bits, col_bits = bits_of(row_count), bits_of(col_count)
    tops = col_count // 2
    lead_pairs = lead // rows // 2

    def other(value, axis, bit):
        count = lax.axis_size(axis)
        return lax.ppermute(value, axis, [(k, k ^ (1 << bit)) for k in range(count)])

    near = packed(features, slot_of_ray, noise)[None]
    own = near
    for bit in reversed(range(1, row_bits)):
        near = jnp.concatenate([near, other(near, "row", bit)])
    high_bits = row_bits - 1 - bits_of(lead_pairs)
    group = reversed_bits(row_index >> (row_bits - high_bits), high_bits)

    def leading(blocks):
        split = blocks.reshape(lead_pairs, 1 << high_bits, *blocks.shape[1:])
        return lax.dynamic_index_in_dim(split, group, 1, False)

    near_x = other(near, "row", 0)
    side = [jnp.concatenate([leading(near), own])]
    side_x = [leading(near_x)]
    for bit in reversed(range(1, col_bits)):
        side += [other(value, "col", bit) for value in side]
        side_x += [other(value, "col", bit) for value in side_x]
    core = [other(value, "col", 0) for value in side]
    core_x = [other(value, "col", 0) for value in side_x]

    cols = col_width - lead // col_count
    padded = -(-cols // PANEL) * PANEL
    rays = lead + rows + padded
    front, factor = pl.pallas_call(
        functools.partial(
            kernel, ray_dev=ray_dev, row_count=row_count, col_count=col_count, lead=lead, tops=tops
        ),
        out_shape=(
            jax.ShapeDtypeStruct((rows, 1, col_width), jnp.float32),
            jax.ShapeDtypeStruct((rows, lead), jnp.float32),
        ),
        scratch_shapes=[
            pltpu.VMEM((rays, features.shape[1]), features.dtype),
            *[pltpu.VMEM((rays // LANES, LANES), jnp.float32)] * 3,
            pltpu.VMEM((lead + rows, lead + padded), jnp.float32),
            pltpu.VMEM((6 * PANEL, lead + padded), jnp.bfloat16),
            pltpu.VMEM((lead + rows, 6 * PANEL), jnp.bfloat16),
        ],
        name="panels",
    )(near, near_x, *side, *side_x, *core, *core_x)
    return front, factor


def solution(mesh):
    return jax.shard_map(
        shards,
        mesh=mesh,
        in_specs=(P(("row", "col"), None), P(("row", "col")), P(("row", "col"))),
        out_specs=(P("row", "col", None), P("row", None)),
        check_vma=False,
    )
```

```python
import functools

import jax
import jax.numpy as jnp
from jax import lax
from jax.experimental import pallas as pl
from jax.experimental.pallas import tpu as pltpu
from jax.sharding import PartitionSpec as P

PANEL = 256
PANELS = 4
NT = 64
LANES = 128
SUBS = 8
HALF = PANEL // 2


def time_rate():
    length = NT / 8.0
    return 1.0 / (2.0 * length * length)


def terms_of(value):
    high = value.astype(jnp.bfloat16)
    rest = value - high.astype(jnp.float32)
    middle = rest.astype(jnp.bfloat16)
    low = (rest - middle.astype(jnp.float32)).astype(jnp.bfloat16)
    return high, middle, low


def left(value):
    high, middle, low = terms_of(value)
    return jnp.concatenate([low, high, middle, middle, high, high], axis=1)


def right(value):
    high, middle, low = terms_of(value)
    return jnp.concatenate([high, low, middle, high, middle, high], axis=0)


def product(a, b):
    return jnp.dot(a, b, preferred_element_type=jnp.float32)


def inverse_factor(block, others=()):
    count = block.shape[0] // SUBS
    per, ahead = count // 2, SUBS // 2
    strips = [block[SUBS * t : SUBS * (t + 1), :] for t in range(count)]
    shape = (SUBS, LANES)
    lane = lax.broadcasted_iota(jnp.int32, shape, 1)
    sub = lax.broadcasted_iota(jnp.int32, shape, 0)

    def over_subs(x, k):
        return jnp.broadcast_to(x[k : k + 1, :], shape)

    def over_lanes(x, j):
        return jnp.broadcast_to(x[:, j : j + 1], shape)

    result = []
    early = []
    for s in range(count):
        for work in others[len(others) * s // count : len(others) * (s + 1) // count]:
            work()
        base = SUBS * s
        end = (s // per + 1) * per
        raw = early + [over_lanes(strips[s], base + j) for j in range(len(early), SUBS)]
        corner = list(raw)
        own = (lane >= base) & (lane < base + SUBS)
        rows = jnp.where(own, jnp.where(lane - base == sub, 1.0, 0.0), strips[s])
        scaled = rows
        pivots = rows
        near = s + 1 < end
        early = []
        if near:
            cols = [over_lanes(strips[s + 1], base + k) for k in range(SUBS)]
            early = [over_lanes(strips[s + 1], base + SUBS + j) for j in range(ahead)]
            following = jnp.where(own, 0.0, strips[s + 1])
        for k in range(0, SUBS, 2):
            here, after = sub == k, sub == k + 1
            a, b, c = over_subs(raw[k], k), over_subs(raw[k], k + 1), over_subs(raw[k + 1], k + 1)
            det = a * c - b * b
            inv_a, inv_det = 1.0 / a, 1.0 / det
            ratio = b * inv_a
            plain = corner[k + 1] - corner[k] * ratio
            second = jnp.where(here, ratio, plain)
            row = over_subs(rows, k) * inv_a
            rows = jnp.where(here, row, rows - corner[k] * row)
            row_2 = (over_subs(rows, k + 1) * a) * inv_det
            rows = jnp.where(after, row_2, rows - second * row_2)
            scaled = jnp.where(here, row, jnp.where(after, row_2, scaled))
            pivots = jnp.where(here, a, jnp.where(after, det * inv_a, pivots))
            entries = []
            for j in range(k + 2, SUBS):
                entry = over_subs(raw[k], j) * inv_a
                entry_2 = over_subs(plain, j) * a
                entries.append((entry, entry_2))
                first = jnp.where(here, entry, corner[j] - corner[k] * entry)
                raw[j] = first - (second * entry_2) * inv_det
                corner[j] = jnp.where(after, entry_2 * inv_det, raw[j])
            if near:
                col = cols[k]
                col_2 = cols[k + 1] - col * ratio
                for j, (entry, entry_2) in zip(range(k + 2, SUBS), entries):
                    cols[j] = (cols[j] - col * entry) - (col_2 * entry_2) * inv_det
                following = (following - col * row) - col_2 * row_2
                for j in range(ahead):
                    part = early[j] - col * (over_subs(col, j) * inv_a)
                    early[j] = part - (col_2 * (over_subs(col_2, j) * a)) * inv_det
        result.append(scaled * jnp.sqrt(pivots))
        if near:
            strips[s + 1] = following
        if s + 2 < end:
            lead_rows = [over_subs(rows, k) for k in range(SUBS)]
        for t in range(s + 2, end):
            parts = [over_lanes(strips[t], base + k) * lead_rows[k] for k in range(SUBS)]
            while len(parts) > 1:
                parts = [x + y for x, y in zip(parts[::2], parts[1::2])]
            strips[t] = jnp.where(own, 0.0, strips[t]) - parts[0]
        if s + 1 == end < count:
            solved = jnp.concatenate(result, axis=0)
            lanes = lax.broadcasted_iota(jnp.int32, solved.shape, 1)
            subs = lax.broadcasted_iota(jnp.int32, solved.shape, 0)
            clean = jnp.where((lanes < SUBS * end) & (lanes > subs), 0.0, solved)
            change = lax.dot_general(
                solved,
                clean,
                (((0,), (0,)), ((), ())),
                precision=lax.Precision.HIGHEST,
                preferred_element_type=jnp.float32,
            )
            for t in range(end, count):
                keep = jnp.where(lane < SUBS * end, 0.0, strips[t])
                strips[t] = keep - change[SUBS * t : SUBS * (t + 1), :]
    result = [jnp.where(lane - SUBS * s <= sub, result[s], 0.0) for s in range(count)]
    return jnp.concatenate(result, axis=0)


def as_column(row):
    return jnp.broadcast_to(row, (LANES, LANES)).T


def reversed_bits(value, bits):
    out = 0
    for k in range(bits):
        out = out | (((value >> k) & 1) << (bits - 1 - k))
    return out


def bits_of(count):
    return count.bit_length() - 1


def kernel(*refs, ray_dev, row_count, col_count, lead, tops):
    near, near_x = refs[:2]
    lists = [refs[2 + k * tops : 2 + (k + 1) * tops] for k in range(4)]
    side, side_x, core, core_x = lists
    front, factor, feat, slot, noise, ray, mat, uppers, lowers_of = refs[2 + 4 * tops :]
    row_index, col_index = lax.axis_index("row"), lax.axis_index("col")
    rows = ray_dev * col_count
    pair_count = near.shape[0]
    lead_pairs = lead // rows // 2
    cols = (pair_count - lead_pairs) * 2 * ray_dev
    row_pair, odd_row = row_index // 2, row_index % 2
    col_pair, odd_col = col_index // 2, col_index % 2
    lanes = lax.broadcasted_iota(jnp.int32, (1, LANES), 1)

    def aux_of(block):
        lines = block[ray_dev : ray_dev + SUBS, 0:LANES].astype(jnp.float32)
        parts = [lines[k : k + 1] for k in range(4)]
        return parts[0], parts[1] + parts[2] + parts[3]

    def put(mine, other, odd, to, numbers):
        here = pl.multiple_of(to + odd * ray_dev, ray_dev)
        there = pl.multiple_of(to + (1 - odd) * ray_dev, ray_dev)
        feat[pl.ds(here, ray_dev), :] = mine[:ray_dev, :]
        feat[pl.ds(there, ray_dev), :] = other[:ray_dev, :]
        tile = to // LANES
        for out, a, b in zip((slot, noise), aux_of(mine), aux_of(other)):
            even, late = jnp.where(odd == 0, a, b), jnp.where(odd == 0, b, a)
            out[pl.ds(tile, 1), :] = even + pltpu.roll(late, ray_dev, 1)
        ray[pl.ds(tile, 1), :] = numbers.astype(jnp.float32)

    low_bits = bits_of(lead_pairs)
    for k in range(lead_pairs):
        pair = (row_pair % lead_pairs) ^ reversed_bits(k, low_bits)
        for bit in range(2):
            row = pair * 2 + (odd_row if bit == 0 else 1 - odd_row)
            for top in range(tops):
                at = (col_pair ^ reversed_bits(top, bits_of(tops))) * LANES + row * rows
                mine, other = (side, core) if bit == 0 else (side_x, core_x)
                put(mine[top][k], other[top][k], odd_col, at, lanes + at)
    for top in range(tops):
        at = (col_pair ^ reversed_bits(top, bits_of(tops))) * LANES
        numbers = lanes + (row_index * rows + at)
        put(side[top][lead_pairs], core[top][lead_pairs], odd_col, lead + at, numbers)
    for place in range(pair_count):
        pair = row_pair ^ reversed_bits(place, bits_of(pair_count))

        @pl.when(pair >= lead_pairs)
        def _():
            numbers = ((pair * 2 + lanes // ray_dev) * col_count + col_index) * ray_dev
            numbers = numbers + lanes % ray_dev
            at = lead + rows + (pair - lead_pairs) * LANES
            put(near[place], near_x[place], odd_row, at, numbers)

    if cols % PANEL:
        feat[lead + rows + cols :, :] = jnp.zeros((PANEL - cols % PANEL, feat.shape[1]), feat.dtype)
        for out in (slot, noise, ray):
            out[(lead + rows + cols) // LANES :, :] = jnp.full((1, LANES), -1.0, jnp.float32)

    panels, row_tiles = lead // PANEL, rows // PANEL
    col_tiles = (cols + PANEL - 1) // PANEL

    skipped = front.shape[2] - cols
    front[:, 0, 0:skipped] = jnp.zeros((rows, skipped), jnp.float32)

    def tile(i):
        start = i * PANEL
        return pl.ds(start if isinstance(start, int) else pl.multiple_of(start, PANEL), PANEL)

    def each(start, count, body):
        if count <= 2:
            return [functools.partial(body, i) for i in range(start, start + count)]

        def loop():
            @pl.loop(start, start + count)
            def _(i):
                body(i)

        return [loop]

    def column(source, i):
        return jnp.concatenate([as_column(source[pl.ds(2 * i + k, 1), :]) for k in range(2)], axis=0)

    def line(source, i):
        return [source[pl.ds(2 * i + k, 1), :] for k in range(2)]

    def fill(i, j, slot_a, ray_a=None):
        at = j if isinstance(j, int) and j < panels else j + row_tiles
        gram = lax.dot_general(
            feat[tile(i), :],
            feat[tile(at), :],
            (((1,), (1,)), ((), ())),
            preferred_element_type=jnp.float32,
        )
        halves = []
        for k, (slot_b, noise_b, ray_b) in enumerate(
            zip(line(slot, at), line(noise, at), line(ray, at))
        ):
            gap = slot_a - slot_b
            part = gram[:, k * LANES : (k + 1) * LANES] * jnp.exp(-gap * gap * time_rate())
            if ray_a is not None:
                part = part + jnp.where(ray_a == ray_b, noise_b, 0.0)
            halves.append(part)
        mat[tile(i), tile(j)] = jnp.concatenate(halves, axis=1)

    columns = {}

    def prepare(i):
        columns[i] = column(slot, i), column(ray, i)

    def fill_lead(i, j):
        fill(i, j, columns[i][0])

    def fill_own(i, j):
        fill(i, j, *columns[i])

    def fills(i):
        found = [functools.partial(fill_lead, i, j) for j in range(i + 1, panels)]
        return found + each(panels, col_tiles, functools.partial(fill_lead, i))

    prepare(0)
    fill_own(0, 0)
    early, late = fills(0), []
    for i in range(1, panels):
        own = [functools.partial(prepare, i), functools.partial(fill_own, i, i)]
        if i == 1:
            early += own
        else:
            late += own
        late += fills(i)
    for i in range(panels, panels + row_tiles):
        late += [functools.partial(prepare, i)]
        late += [functools.partial(fill_own, i, j) for j in range(panels)]
        late += each(panels, col_tiles, functools.partial(fill_own, i))

    half = 6 * HALF

    for p in range(panels):
        upper, lowers = uppers.at[p % uppers.shape[0]], lowers_of.at[p % uppers.shape[0]]
        top, low = pl.ds(p * PANEL, HALF), pl.ds(p * PANEL + HALF, HALF)
        inv_a = inverse_factor(mat[top, top], early)
        left_a = left(inv_a)
        cross = product(left_a, right(mat[top, low]))
        cross_left, cross_right = left(cross.T), right(cross)
        corner = mat[low, low] - product(cross_left, cross_right)

        def solve_top(j, upper=upper, left_a=left_a, cross_left=cross_left, top=top, low=low):
            found = product(left_a, right(mat[top, tile(j)]))
            terms = right(found)
            upper[0:half, tile(j)] = terms
            mat[low, tile(j)] -= product(cross_left, terms)
            return found

        if p + 1 < panels:
            lowers[tile(p + 1), 0:half] = left(solve_top(p + 1).T)
            mat[tile(p + 1), tile(p + 1)] -= product(
                lowers[tile(p + 1), 0:half], upper[0:half, tile(p + 1)]
            )

        def top_of(j, lowers=lowers, solve_top=solve_top):
            lowers[tile(j), 0:half] = left(solve_top(j).T)

        late = late + [functools.partial(top_of, j) for j in range(p + 2, panels)]
        inv_b = inverse_factor(corner, late + each(panels, col_tiles, solve_top))
        left_b = left(inv_b)

        def solve_low(j, upper=upper, left_b=left_b, low=low):
            found = product(left_b, right(mat[low, tile(j)]))
            upper[half:, tile(j)] = right(found)
            return found

        def low_of(j, lowers=lowers, solve_low=solve_low):
            lowers[tile(j), half:] = left(solve_low(j).T)

        if p + 1 < panels:
            low_of(p + 1)
            mat[tile(p + 1), tile(p + 1)] -= product(
                lowers[tile(p + 1), half:], upper[half:, tile(p + 1)]
            )

        def solve_row(
            i, p=p, top=top, low=low, inv_a=inv_a, inv_b=inv_b, cross_right=cross_right, lowers=lowers
        ):
            row = tile(panels + i)
            first = product(left(mat[row, top]), right(inv_a.T))
            first_left = left(first)
            second = product(left(mat[row, low] - product(first_left, cross_right)), right(inv_b.T))
            ray_a = column(ray, panels + i)
            kept = [
                jnp.where(ray_a >= ray_b, part, 0.0)
                for part, ray_b in zip((first, second), line(ray, p))
            ]
            factor[tile(i), tile(p)] = jnp.concatenate(kept, axis=1)
            lowers[row, 0:half] = first_left
            lowers[row, half:] = left(second)

        def update(start, count, j, upper=upper, lowers=lowers):
            some = pl.ds(start * PANEL, count * PANEL)
            mat[some, tile(j)] -= product(lowers[some, :], upper[:, tile(j)])

        rest = panels + row_tiles
        early = [functools.partial(low_of, j) for j in range(p + 2, panels)]
        early += each(panels, col_tiles, solve_low)
        late = each(0, row_tiles, solve_row)
        if p + 1 < panels:
            early += [functools.partial(update, p + 1, 1, j) for j in range(p + 2, panels)]
            early += each(panels, col_tiles, functools.partial(update, p + 1, 1))
            late += [
                functools.partial(update, p + 2, j - p - 1, j) for j in range(p + 2, panels)
            ]
            late += [functools.partial(update, panels, row_tiles, j) for j in range(p + 1, panels)]
        late += each(panels, col_tiles, functools.partial(update, p + 2, rest - p - 2) if p + 1 < panels
            else functools.partial(update, panels, row_tiles))
        if uppers.shape[0] == 1 and p + 1 < panels:
            early, late = early + late, []
    for work in early + late:
        work()

    front[:, 0, skipped:] = jnp.where(
        row_index * rows >= lead, mat[lead : lead + rows, lead : lead + cols], 0.0
    )


def packed(features, slot_of_ray, noise):
    high = lax.reduce_precision(noise, 8, 7)
    middle = lax.reduce_precision(noise - high, 8, 7)
    terms = jnp.stack([slot_of_ray.astype(jnp.float32), high, middle, noise - high - middle])
    ray_dev, width = features.shape
    aux = jnp.pad(terms, ((0, SUBS - 4), (0, width - ray_dev))).astype(features.dtype)
    return jnp.concatenate([features, aux])


def shards(features, slot_of_ray, noise):
    ray_dev = noise.shape[0]
    row_count, col_count = lax.axis_size("row"), lax.axis_size("col")
    rows, col_width = ray_dev * col_count, ray_dev * row_count
    row_index = lax.axis_index("row")
    lead = PANELS * PANEL
    row_bits, col_bits = bits_of(row_count), bits_of(col_count)
    tops = col_count // 2
    lead_pairs = lead // rows // 2

    def other(value, axis, bit):
        count = lax.axis_size(axis)
        return lax.ppermute(value, axis, [(k, k ^ (1 << bit)) for k in range(count)])

    near = packed(features, slot_of_ray, noise)[None]
    own = near
    for bit in reversed(range(1, row_bits)):
        near = jnp.concatenate([near, other(near, "row", bit)])
    high_bits = row_bits - 1 - bits_of(lead_pairs)
    group = reversed_bits(row_index >> (row_bits - high_bits), high_bits)

    def leading(blocks):
        split = blocks.reshape(lead_pairs, 1 << high_bits, *blocks.shape[1:])
        return lax.dynamic_index_in_dim(split, group, 1, False)

    near_x = other(near, "row", 0)
    side = [jnp.concatenate([leading(near), own])]
    side_x = [leading(near_x)]
    for bit in reversed(range(1, col_bits)):
        side += [other(value, "col", bit) for value in side]
        side_x += [other(value, "col", bit) for value in side_x]
    core = [other(value, "col", 0) for value in side]
    core_x = [other(value, "col", 0) for value in side_x]

    cols = col_width - lead // col_count
    padded = -(-cols // PANEL) * PANEL
    rays = lead + rows + padded
    sets = 2 if padded <= 2 * PANEL else 1
    front, factor = pl.pallas_call(
        functools.partial(
            kernel, ray_dev=ray_dev, row_count=row_count, col_count=col_count, lead=lead, tops=tops
        ),
        out_shape=(
            jax.ShapeDtypeStruct((rows, 1, col_width), jnp.float32),
            jax.ShapeDtypeStruct((rows, lead), jnp.float32),
        ),
        scratch_shapes=[
            pltpu.VMEM((rays, features.shape[1]), features.dtype),
            *[pltpu.VMEM((rays // LANES, LANES), jnp.float32)] * 3,
            pltpu.VMEM((lead + rows, lead + padded), jnp.float32),
            pltpu.VMEM((sets, 6 * PANEL, lead + padded), jnp.bfloat16),
            pltpu.VMEM((sets, lead + rows, 6 * PANEL), jnp.bfloat16),
        ],
        name="panels",
    )(near, near_x, *side, *side_x, *core, *core_x)
    return front, factor


def solution(mesh):
    return jax.shard_map(
        shards,
        mesh=mesh,
        in_specs=(P(("row", "col"), None), P(("row", "col")), P(("row", "col"))),
        out_specs=(P("row", "col", None), P("row", None)),
        check_vma=False,
    )
```

```python
import functools

import jax
import jax.numpy as jnp
from jax import lax
from jax.experimental import pallas as pl
from jax.experimental.pallas import tpu as pltpu
from jax.sharding import PartitionSpec as P

PANEL = 256
PANELS = 4
NT = 64
LANES = 128
SUBS = 8
HALF = PANEL // 2


def time_rate():
    length = NT / 8.0
    return 1.0 / (2.0 * length * length)


def terms_of(value):
    high = value.astype(jnp.bfloat16)
    rest = value - high.astype(jnp.float32)
    middle = rest.astype(jnp.bfloat16)
    low = (rest - middle.astype(jnp.float32)).astype(jnp.bfloat16)
    return high, middle, low


def left(value):
    high, middle, low = terms_of(value)
    return jnp.concatenate([low, high, middle, middle, high, high], axis=1)


def right(value):
    high, middle, low = terms_of(value)
    return jnp.concatenate([high, low, middle, high, middle, high], axis=0)


def product(a, b):
    return jnp.dot(a, b, preferred_element_type=jnp.float32)


def inverse_factor(block, others=()):
    count = block.shape[0] // SUBS
    per, ahead = count // 2, SUBS // 2
    strips = [block[SUBS * t : SUBS * (t + 1), :] for t in range(count)]
    shape = (SUBS, LANES)
    lane = lax.broadcasted_iota(jnp.int32, shape, 1)
    sub = lax.broadcasted_iota(jnp.int32, shape, 0)

    def over_subs(x, k):
        return jnp.broadcast_to(x[k : k + 1, :], shape)

    def over_lanes(x, j):
        return jnp.broadcast_to(x[:, j : j + 1], shape)

    result = []
    early = []
    for s in range(count):
        for work in others[len(others) * s // count : len(others) * (s + 1) // count]:
            work()
        base = SUBS * s
        end = (s // per + 1) * per
        raw = early + [over_lanes(strips[s], base + j) for j in range(len(early), SUBS)]
        corner = list(raw)
        own = (lane >= base) & (lane < base + SUBS)
        rows = jnp.where(own, jnp.where(lane - base == sub, 1.0, 0.0), strips[s])
        scaled = rows
        pivots = rows
        near = s + 1 < end
        early = []
        if near:
            cols = [over_lanes(strips[s + 1], base + k) for k in range(SUBS)]
            early = [over_lanes(strips[s + 1], base + SUBS + j) for j in range(ahead)]
            following = jnp.where(own, 0.0, strips[s + 1])
        for k in range(0, SUBS, 2):
            here, after = sub == k, sub == k + 1
            a, b, c = over_subs(raw[k], k), over_subs(raw[k], k + 1), over_subs(raw[k + 1], k + 1)
            det = a * c - b * b
            inv_a, inv_det = 1.0 / a, 1.0 / det
            ratio = b * inv_a
            plain = corner[k + 1] - corner[k] * ratio
            second = jnp.where(here, ratio, plain)
            row = over_subs(rows, k) * inv_a
            rows = jnp.where(here, row, rows - corner[k] * row)
            row_2 = (over_subs(rows, k + 1) * a) * inv_det
            rows = jnp.where(after, row_2, rows - second * row_2)
            scaled = jnp.where(here, row, jnp.where(after, row_2, scaled))
            pivots = jnp.where(here, a, jnp.where(after, det * inv_a, pivots))
            entries = []
            for j in range(k + 2, SUBS):
                entry = over_subs(raw[k], j) * inv_a
                entry_2 = over_subs(plain, j) * a
                entries.append((entry, entry_2))
                first = jnp.where(here, entry, corner[j] - corner[k] * entry)
                raw[j] = first - (second * entry_2) * inv_det
                corner[j] = jnp.where(after, entry_2 * inv_det, raw[j])
            if near:
                col = cols[k]
                col_2 = cols[k + 1] - col * ratio
                for j, (entry, entry_2) in zip(range(k + 2, SUBS), entries):
                    cols[j] = (cols[j] - col * entry) - (col_2 * entry_2) * inv_det
                following = (following - col * row) - col_2 * row_2
                for j in range(ahead):
                    part = early[j] - col * (over_subs(col, j) * inv_a)
                    early[j] = part - (col_2 * (over_subs(col_2, j) * a)) * inv_det
        result.append(scaled * jnp.sqrt(pivots))
        if near:
            strips[s + 1] = following
        if s + 2 < end:
            lead_rows = [over_subs(rows, k) for k in range(SUBS)]
        for t in range(s + 2, end):
            parts = [over_lanes(strips[t], base + k) * lead_rows[k] for k in range(SUBS)]
            while len(parts) > 1:
                parts = [x + y for x, y in zip(parts[::2], parts[1::2])]
            strips[t] = jnp.where(own, 0.0, strips[t]) - parts[0]
        if s + 1 == end < count:
            solved = jnp.concatenate(result, axis=0)
            lanes = lax.broadcasted_iota(jnp.int32, solved.shape, 1)
            subs = lax.broadcasted_iota(jnp.int32, solved.shape, 0)
            clean = jnp.where((lanes < SUBS * end) & (lanes > subs), 0.0, solved)
            change = lax.dot_general(
                solved,
                clean,
                (((0,), (0,)), ((), ())),
                precision=lax.Precision.HIGHEST,
                preferred_element_type=jnp.float32,
            )
            for t in range(end, count):
                keep = jnp.where(lane < SUBS * end, 0.0, strips[t])
                strips[t] = keep - change[SUBS * t : SUBS * (t + 1), :]
    result = [jnp.where(lane - SUBS * s <= sub, result[s], 0.0) for s in range(count)]
    return jnp.concatenate(result, axis=0)


def as_column(row):
    return jnp.broadcast_to(row, (LANES, LANES)).T


def reversed_bits(value, bits):
    out = 0
    for k in range(bits):
        out = out | (((value >> k) & 1) << (bits - 1 - k))
    return out


def bits_of(count):
    return count.bit_length() - 1


def kernel(*refs, ray_dev, row_count, col_count, lead, tops):
    near, near_x = refs[:2]
    lists = [refs[2 + k * tops : 2 + (k + 1) * tops] for k in range(4)]
    side, side_x, core, core_x = lists
    front, factor, feat, slot, noise, ray, mat, uppers, lowers_of = refs[2 + 4 * tops :]
    row_index, col_index = lax.axis_index("row"), lax.axis_index("col")
    rows = ray_dev * col_count
    pair_count = near.shape[0]
    lead_pairs = lead // rows // 2
    cols = (pair_count - lead_pairs) * 2 * ray_dev
    row_pair, odd_row = row_index // 2, row_index % 2
    col_pair, odd_col = col_index // 2, col_index % 2
    lanes = lax.broadcasted_iota(jnp.int32, (1, LANES), 1)

    def aux_of(block):
        lines = block[ray_dev : ray_dev + SUBS, 0:LANES].astype(jnp.float32)
        parts = [lines[k : k + 1] for k in range(4)]
        return parts[0], parts[1] + parts[2] + parts[3]

    def put(mine, other, odd, to, numbers):
        here = pl.multiple_of(to + odd * ray_dev, ray_dev)
        there = pl.multiple_of(to + (1 - odd) * ray_dev, ray_dev)
        feat[pl.ds(here, ray_dev), :] = mine[:ray_dev, :]
        feat[pl.ds(there, ray_dev), :] = other[:ray_dev, :]
        tile = to // LANES
        for out, a, b in zip((slot, noise), aux_of(mine), aux_of(other)):
            even, late = jnp.where(odd == 0, a, b), jnp.where(odd == 0, b, a)
            out[pl.ds(tile, 1), :] = even + pltpu.roll(late, ray_dev, 1)
        ray[pl.ds(tile, 1), :] = numbers.astype(jnp.float32)

    low_bits = bits_of(lead_pairs)
    for k in range(lead_pairs):
        pair = (row_pair % lead_pairs) ^ reversed_bits(k, low_bits)
        for bit in range(2):
            row = pair * 2 + (odd_row if bit == 0 else 1 - odd_row)
            for top in range(tops):
                at = (col_pair ^ reversed_bits(top, bits_of(tops))) * LANES + row * rows
                mine, other = (side, core) if bit == 0 else (side_x, core_x)
                put(mine[top][k], other[top][k], odd_col, at, lanes + at)
    for top in range(tops):
        at = (col_pair ^ reversed_bits(top, bits_of(tops))) * LANES
        numbers = lanes + (row_index * rows + at)
        put(side[top][lead_pairs], core[top][lead_pairs], odd_col, lead + at, numbers)
    for place in range(pair_count):
        pair = row_pair ^ reversed_bits(place, bits_of(pair_count))

        @pl.when(pair >= lead_pairs)
        def _():
            numbers = ((pair * 2 + lanes // ray_dev) * col_count + col_index) * ray_dev
            numbers = numbers + lanes % ray_dev
            at = lead + rows + (pair - lead_pairs) * LANES
            put(near[place], near_x[place], odd_row, at, numbers)

    if cols % PANEL:
        feat[lead + rows + cols :, :] = jnp.zeros((PANEL - cols % PANEL, feat.shape[1]), feat.dtype)
        for out in (slot, noise, ray):
            out[(lead + rows + cols) // LANES :, :] = jnp.full((1, LANES), -1.0, jnp.float32)

    panels, row_tiles = lead // PANEL, rows // PANEL
    col_tiles = (cols + PANEL - 1) // PANEL

    skipped = front.shape[2] - cols
    front[:, 0, 0:skipped] = jnp.zeros((rows, skipped), jnp.float32)

    def tile(i):
        start = i * PANEL
        return pl.ds(start if isinstance(start, int) else pl.multiple_of(start, PANEL), PANEL)

    def each(start, count, body):
        if count <= 2:
            return [functools.partial(body, i) for i in range(start, start + count)]

        def loop():
            @pl.loop(start, start + count)
            def _(i):
                body(i)

        return [loop]

    def column(source, i):
        return jnp.concatenate([as_column(source[pl.ds(2 * i + k, 1), :]) for k in range(2)], axis=0)

    def line(source, i):
        return [source[pl.ds(2 * i + k, 1), :] for k in range(2)]

    def fill(i, j, slot_a, ray_a=None):
        at = j if isinstance(j, int) and j < panels else j + row_tiles
        gram = lax.dot_general(
            feat[tile(i), :],
            feat[tile(at), :],
            (((1,), (1,)), ((), ())),
            preferred_element_type=jnp.float32,
        )
        halves = []
        for k, (slot_b, noise_b, ray_b) in enumerate(
            zip(line(slot, at), line(noise, at), line(ray, at))
        ):
            gap = slot_a - slot_b
            part = gram[:, k * LANES : (k + 1) * LANES] * jnp.exp(-gap * gap * time_rate())
            if ray_a is not None:
                part = part + jnp.where(ray_a == ray_b, noise_b, 0.0)
            halves.append(part)
        mat[tile(i), tile(j)] = jnp.concatenate(halves, axis=1)

    columns = {}

    def prepare(i):
        columns[i] = column(slot, i), column(ray, i)

    def fill_lead(i, j):
        fill(i, j, columns[i][0])

    def fill_own(i, j):
        fill(i, j, *columns[i])

    def fills(i):
        found = [functools.partial(fill_lead, i, j) for j in range(i + 1, panels)]
        return found + each(panels, col_tiles, functools.partial(fill_lead, i))

    prepare(0)
    fill_own(0, 0)
    early, late = fills(0), []
    for i in range(1, panels):
        own = [functools.partial(prepare, i), functools.partial(fill_own, i, i)]
        if i == 1:
            early += own
        else:
            late += own
        late += fills(i)
    for i in range(panels, panels + row_tiles):
        late += [functools.partial(prepare, i)]
        late += [functools.partial(fill_own, i, j) for j in range(panels)]
        late += each(panels, col_tiles, functools.partial(fill_own, i))

    half = 6 * HALF

    for p in range(panels):
        upper, lowers = uppers.at[p % uppers.shape[0]], lowers_of.at[p % uppers.shape[0]]
        top, low = pl.ds(p * PANEL, HALF), pl.ds(p * PANEL + HALF, HALF)
        inv_a = inverse_factor(mat[top, top], early)
        left_a = left(inv_a)
        cross = product(left_a, right(mat[top, low]))
        cross_left, cross_right = left(cross.T), right(cross)
        corner = mat[low, low] - product(cross_left, cross_right)

        def solve_top(j, upper=upper, left_a=left_a, cross_left=cross_left, top=top, low=low):
            found = product(left_a, right(mat[top, tile(j)]))
            terms = right(found)
            upper[0:half, tile(j)] = terms
            mat[low, tile(j)] -= product(cross_left, terms)
            return found

        if p + 1 < panels:
            lowers[tile(p + 1), 0:half] = left(solve_top(p + 1).T)
            mat[tile(p + 1), tile(p + 1)] -= product(
                lowers[tile(p + 1), 0:half], upper[0:half, tile(p + 1)]
            )

        def top_of(j, lowers=lowers, solve_top=solve_top):
            lowers[tile(j), 0:half] = left(solve_top(j).T)

        late = late + [functools.partial(top_of, j) for j in range(p + 2, panels)]
        inv_b = inverse_factor(corner, late + each(panels, col_tiles, solve_top))
        left_b = left(inv_b)

        def solve_low(j, upper=upper, left_b=left_b, low=low):
            found = product(left_b, right(mat[low, tile(j)]))
            upper[half:, tile(j)] = right(found)
            return found

        def low_of(j, lowers=lowers, solve_low=solve_low):
            lowers[tile(j), half:] = left(solve_low(j).T)

        if p + 1 < panels:
            low_of(p + 1)
            mat[tile(p + 1), tile(p + 1)] -= product(
                lowers[tile(p + 1), half:], upper[half:, tile(p + 1)]
            )

        def solve_row(
            i, p=p, top=top, low=low, inv_a=inv_a, inv_b=inv_b, cross_right=cross_right, lowers=lowers
        ):
            row = tile(panels + i)
            first = product(left(mat[row, top]), right(inv_a.T))
            first_left = left(first)
            second = product(left(mat[row, low] - product(first_left, cross_right)), right(inv_b.T))
            ray_a = column(ray, panels + i)
            kept = [
                jnp.where(ray_a >= ray_b, part, 0.0)
                for part, ray_b in zip((first, second), line(ray, p))
            ]
            factor[tile(i), tile(p)] = jnp.concatenate(kept, axis=1)
            lowers[row, 0:half] = first_left
            lowers[row, half:] = left(second)

        def update(start, count, j, upper=upper, lowers=lowers):
            some = pl.ds(start * PANEL, count * PANEL)
            mat[some, tile(j)] -= product(lowers[some, :], upper[:, tile(j)])

        rest = panels + row_tiles
        early = [functools.partial(low_of, j) for j in range(p + 2, panels)]
        early += each(panels, col_tiles, solve_low)
        late = each(0, row_tiles, solve_row)
        if p + 1 < panels:
            early += [functools.partial(update, p + 1, 1, j) for j in range(p + 2, panels)]
            early += each(panels, col_tiles, functools.partial(update, p + 1, 1))
            late += [
                functools.partial(update, p + 2, j - p - 1, j) for j in range(p + 2, panels)
            ]
            late += [functools.partial(update, panels, row_tiles, j) for j in range(p + 1, panels)]
        late += each(panels, col_tiles, functools.partial(update, p + 2, rest - p - 2) if p + 1 < panels
            else functools.partial(update, panels, row_tiles))
        if uppers.shape[0] == 1 and p + 1 < panels:
            early, late = early + late, []
    for work in early + late:
        work()

    front[:, 0, skipped:] = jnp.where(
        row_index * rows >= lead, mat[lead : lead + rows, lead : lead + cols], 0.0
    )


def packed(features, slot_of_ray, noise):
    high = lax.reduce_precision(noise, 8, 7)
    middle = lax.reduce_precision(noise - high, 8, 7)
    terms = jnp.stack([slot_of_ray.astype(jnp.float32), high, middle, noise - high - middle])
    ray_dev, width = features.shape
    aux = jnp.pad(terms, ((0, SUBS - 4), (0, width - ray_dev))).astype(features.dtype)
    return jnp.concatenate([features, aux])


def shards(features, slot_of_ray, noise):
    ray_dev = noise.shape[0]
    row_count, col_count = lax.axis_size("row"), lax.axis_size("col")
    rows, col_width = ray_dev * col_count, ray_dev * row_count
    row_index = lax.axis_index("row")
    lead = PANELS * PANEL
    row_bits, col_bits = bits_of(row_count), bits_of(col_count)
    tops = col_count // 2
    lead_pairs = lead // rows // 2

    def other(value, axis, bit):
        count = lax.axis_size(axis)
        return lax.ppermute(value, axis, [(k, k ^ (1 << bit)) for k in range(count)])

    near = packed(features, slot_of_ray, noise)[None]
    own = near
    if row_bits <= 3:
        pairs = row_count // 2
        steps = [2 * reversed_bits(k, row_bits - 1) for k in range(1, pairs)]
        direct = {
            step: lax.ppermute(own, "row", [(k, k ^ step) for k in range(row_count)])
            for step in sorted(steps, reverse=True)
        }
        near = jnp.concatenate([own] + [direct[step] for step in steps])
    else:
        for bit in reversed(range(1, row_bits)):
            near = jnp.concatenate([near, other(near, "row", bit)])
    high_bits = row_bits - 1 - bits_of(lead_pairs)
    group = reversed_bits(row_index >> (row_bits - high_bits), high_bits)

    def leading(blocks):
        split = blocks.reshape(lead_pairs, 1 << high_bits, *blocks.shape[1:])
        return lax.dynamic_index_in_dim(split, group, 1, False)

    near_x = other(near, "row", 0)
    side = [jnp.concatenate([leading(near), own])]
    side_x = [leading(near_x)]
    for bit in reversed(range(1, col_bits)):
        side += [other(value, "col", bit) for value in side]
        side_x += [other(value, "col", bit) for value in side_x]
    core = [other(value, "col", 0) for value in side]
    core_x = [other(value, "col", 0) for value in side_x]

    cols = col_width - lead // col_count
    padded = -(-cols // PANEL) * PANEL
    rays = lead + rows + padded
    sets = 2 if padded <= 2 * PANEL else 1
    front, factor = pl.pallas_call(
        functools.partial(
            kernel, ray_dev=ray_dev, row_count=row_count, col_count=col_count, lead=lead, tops=tops
        ),
        out_shape=(
            jax.ShapeDtypeStruct((rows, 1, col_width), jnp.float32),
            jax.ShapeDtypeStruct((rows, lead), jnp.float32),
        ),
        scratch_shapes=[
            pltpu.VMEM((rays, features.shape[1]), features.dtype),
            *[pltpu.VMEM((rays // LANES, LANES), jnp.float32)] * 3,
            pltpu.VMEM((lead + rows, lead + padded), jnp.float32),
            pltpu.VMEM((sets, 6 * PANEL, lead + padded), jnp.bfloat16),
            pltpu.VMEM((sets, lead + rows, 6 * PANEL), jnp.bfloat16),
        ],
        name="panels",
    )(near, near_x, *side, *side_x, *core, *core_x)
    return front, factor


def solution(mesh):
    return jax.shard_map(
        shards,
        mesh=mesh,
        in_specs=(P(("row", "col"), None), P(("row", "col")), P(("row", "col"))),
        out_specs=(P("row", "col", None), P("row", None)),
        check_vma=False,
    )
```
